128 devices in a mesh: dp: 16 (over x, y), expert: 8 (over z, core).
Axes of the slice: x: 4, y: 4, z: 4, core: 2. Of those that a mesh axis runs over, the one named last changes fastest.
Arguments:
- residual: bfloat16 [1024, 4096], P('dp', 'expert'), may hold values from -6 to 6
- queries: bfloat16 [1024, 4096], P('dp', 'expert'), may hold values from -25 to 25
- cache_keys: bfloat16 [36864, 1024], P('dp', 'expert'), may hold values from -5 to 5
- cache_values: bfloat16 [36864, 1024], P('dp', 'expert'), may hold values from -18 to 18
- node_of_position: int32 [36864], P('dp'), may hold values from -1 to 36, as said below
- parent: int32 [37], replicated, may hold values from 0 to 4, as said below
- leaf_ids: int32 [1024], P('dp'), may hold values from 5 to 36
- routes: int32 [1024, 2], P('dp'), may hold values from 0 to 7, all different within a row; in each aligned block of 64 rows (0 to 63, 64 to 127, ...) at most 32 rows name the same one
- gate_weights: bfloat16 [1024, 2], P('dp'), may hold values from 0.19921875 to 0.796875
- norm_gain: bfloat16 [4096], replicated, may hold values from 0.5 to 1.5
- w_gate: bfloat16 [8, 4096, 14336], P('expert', None, 'dp'), may hold values from -0.09375 to 0.09375
- w_up: bfloat16 [8, 4096, 14336], P('expert', None, 'dp'), may hold values from -0.09375 to 0.09375
- w_down: bfloat16 [8, 14336, 4096], P('expert', 'dp'), may hold values from -0.046875 to 0.046875
Outputs:
- attention_out: bfloat16 [1024, 4096], P('dp', 'expert')
- layer_out: bfloat16 [1024, 4096], P('dp', 'expert')
The draws below stay inside these ranges and needn't reach their ends.
Inputs may be any that keep to these rules, and one draw needn't show every extreme that they name: `node_of_position`: each block of 2304 positions begins with 256 positions of node 0, the root; the rest come in blocks of 128 positions, each holding one non-root node on a leading run of one or more positions and -1 after it; every non-root node holds one or more blocks. Node 0 is the root and its own parent; nodes 1 to 4 have parent 0; the other nodes are leaves with a parent among nodes 1 to 4. `leaf_ids`: every request sits at a leaf. `routes`: the two experts of a request differ; among the 64 requests of one index of dp no expert is named more than 32 times.
All inputs are finite; a program needn't handle non-finite values.
Results may differ from the reference program's by a relative error of at most 0.012.
Values may be sent and summed in bfloat16 or wider, within the bound.
No kernel may reach another device: no remote copies, remote signals or barrier semaphores. Data moves between devices by JAX's collectives and lax.ppermute only.
A program may use at most 128 MiB of HBM per device.

```python
import math
import jax
import jax.numpy as jnp
import numpy as np
from jax import lax

D = 4096
Q_HEADS = 32
KV_HEADS = 8
HEAD_DIM = 128
FF = 14336
EXPERTS = 8
ROWS_DP = 64
ROOT_DEV = 256
BLOCKS_DEV = 16
BLOCK = 128
MIDS = 4
TOKENS = 1024
CACHE_DEV = 2304
CACHE = 36864
NODES = 37
CAP = 32
N_DP = 16


def draw_queries(key, part):
    base_key = jax.random.fold_in(key, 11)
    values = 2.0 * jax.random.truncated_normal(base_key, -4.0, 4.0, (TOKENS, D), jnp.float32)
    return values.astype(jnp.bfloat16)


def draw_cache_keys(key, part):
    base_key = jax.random.fold_in(key, 23)
    values = jax.random.truncated_normal(base_key, -5.0, 5.0, (CACHE, KV_HEADS * HEAD_DIM), jnp.float32)
    return values.astype(jnp.bfloat16)


def draw_node_of_position(key, part):
    device_count = CACHE // CACHE_DEV
    block_count = device_count * BLOCKS_DEV
    block_order = jax.random.permutation(jax.random.fold_in(key, 31), block_count)
    owner_node = 1 + block_order % (NODES - 1)
    used_len = jax.random.randint(jax.random.fold_in(key, 37), (block_count,), 1, BLOCK + 1)
    used_len = jnp.where(block_order == 0, BLOCK, used_len)
    used_len = jnp.where(block_order == 1, 1, used_len)
    local_pos = jnp.arange(CACHE_DEV)
    offset = local_pos - ROOT_DEV
    block_local = jnp.maximum(offset, 0) // BLOCK
    within = jnp.maximum(offset, 0) % BLOCK
    device_ids = jnp.arange(device_count)
    block_ids = device_ids[:, None] * BLOCKS_DEV + block_local[None, :]
    node_ids = jnp.where(within[None, :] < used_len[block_ids], owner_node[block_ids], -1)
    node_ids = jnp.where(offset[None, :] < 0, 0, node_ids)
    return node_ids.reshape(CACHE).astype(jnp.int32)


def draw_parent(key, part):
    node_ids = jnp.arange(NODES)
    chosen = 1 + jax.random.randint(jax.random.fold_in(key, 41), (NODES,), 0, MIDS)
    chosen = jnp.where(node_ids == MIDS + 1, MIDS, chosen)
    return jnp.where(node_ids <= MIDS, 0, chosen).astype(jnp.int32)


def touch_ends(values, own_key, smallest, largest):
    longest = values.shape.index(max(values.shape))
    spots = []
    for shift in (0, 1):
        where = [jax.random.randint(jax.random.fold_in(own_key, axis), (), 0, length) for axis, length in enumerate(values.shape)]
        where[longest] = (where[longest] + shift) % values.shape[longest]
        spots.append(tuple(where))
    return values.at[spots[0]].set(smallest).at[spots[1]].set(largest)


def level_of(key, dims, shards, low, largest):
    level = 1.0
    for dim, blocks in shards:
        heights = jax.random.uniform(jax.random.fold_in(jax.random.fold_in(key, 6), dim), (blocks,), jnp.float32, low / len(shards), largest / len(shards))
        level = level * jnp.repeat(jnp.exp(heights), dims[dim] // blocks).reshape((-1,) + (1,) * (len(dims) - 1 - dim))
    return level


def routed_block(rng, own, number, rows, amount, top, bound, slope):
    ranking = jax.random.permutation(rng, amount)
    heavy_load, usual = shares(amount, rows * top, bound, slope, True), shares(amount, rows * top, bound, slope, False)
    places = jnp.arange(amount)

    def named(tallies, offset_by):
        used = int((tallies > 0).sum())
        fixed = max(1, used // 4)
        shifted = fixed + (places - fixed + offset_by * (used - fixed)) % max(1, amount - fixed)
        return jnp.zeros((amount,), jnp.int32).at[ranking[jnp.where(places < fixed, places, shifted)]].set(jnp.asarray(tallies, jnp.int32))

    tallies = jnp.where(number % 4 == 0, named(heavy_load, number // 4), named(usual, number - number // 4 - 1))
    mixed = jax.random.permutation(jax.random.fold_in(own, 3), amount)
    giver, sink = mixed[0:amount // 2 * 2:2], mixed[1:amount // 2 * 2:2]
    room = jnp.minimum(tallies[giver] - 1, bound - tallies[sink]) // 2
    room = jnp.where((giver == ranking[0]) | (sink == ranking[0]) | (tallies[sink] == 0), 0, jnp.maximum(room, 0))
    shifted = jax.random.randint(jax.random.fold_in(own, 4), (amount // 2,), 0, 1 << 20) % (room + 1)
    tallies = tallies.at[giver].add(-shifted).at[sink].add(shifted)
    members = jnp.searchsorted(jnp.cumsum(tallies), jnp.arange(rows * top), side="right").astype(jnp.int32)
    listing = members.reshape(top, rows).T
    listing = listing[jax.random.permutation(jax.random.fold_in(own, 1), rows)]
    offset_by = jax.random.randint(jax.random.fold_in(own, 2), (rows, 1), 0, top)
    return jnp.take_along_axis(listing, (jnp.arange(top)[None, :] + offset_by) % top, axis=1)


def shares(number_of, total, most, lean, full):
    loads = [(1 << 20) // math.isqrt(rank ** lean) + 1 for rank in range(1, number_of + 1)]
    largest = most if full else min(most, max(-(-total // number_of), total * loads[0] // sum(loads)))
    least = 1 if total - largest >= number_of - 1 else 0
    holding, spare = [largest] + [least] * (number_of - 1), total - largest - least * (number_of - 1)
    while spare > 0:
        candidates = [i for i in range(1, number_of) if holding[i] < largest] or [i for i in range(1, number_of) if holding[i] < most]
        mass, left = sum([loads[i] for i in candidates]), spare
        for i in candidates:
            addition = min(most - holding[i], max(1, left * loads[i] // mass), spare)
            holding[i] = holding[i] + addition
            spare = spare - addition
    return np.array(holding)


def bell_draw(own_key, extent, width, reach, split=(), kind=jnp.bfloat16):
    level = level_of(own_key, extent, split, -0.22, 0.18) if split else 1.0
    entries = jax.random.normal(own_key, extent, jnp.float32) * width * level
    return jnp.minimum(jnp.maximum(entries, -reach), reach).astype(kind)


def setup_inputs(seed: int = 0) -> dict:
    seeds = jax.random.split(jax.random.key(seed), 14)
    residual = bell_draw(seeds[0], (TOKENS, D), 1.0, 6.0, ((0, 16), (1, 8)))
    queries = draw_queries(jax.random.fold_in(seeds[13], 71), 0)
    cache_keys = draw_cache_keys(jax.random.fold_in(seeds[13], 71), 0)
    cache_values = bell_draw(seeds[3], (CACHE, KV_HEADS * HEAD_DIM), 3.0, 18.0, ((0, 16), (1, 8)))
    node_of_position = draw_node_of_position(jax.random.fold_in(seeds[13], 71), 0)
    parent = draw_parent(jax.random.fold_in(seeds[13], 71), 0)
    leaf_ids = touch_ends(jax.random.randint(seeds[6], (TOKENS,), MIDS + 1, NODES), jax.random.fold_in(seeds[6], 1), MIDS + 1, NODES - 1).astype(jnp.int32)
    routes_keys = jax.random.split(jax.random.fold_in(seeds[7], 1), TOKENS // ROWS_DP)
    routes_turns = jax.random.permutation(jax.random.fold_in(seeds[7], 3), TOKENS // ROWS_DP)
    routes = jax.vmap(lambda own, number: routed_block(jax.random.fold_in(seeds[7], 2), own, number, ROWS_DP, EXPERTS, 2, CAP, 2))(routes_keys, routes_turns).reshape((TOKENS, 2))
    gate_weights = jnp.clip(0.19921875 + 0.59765625 * jax.random.uniform(seeds[8], (TOKENS, 2), jnp.float32) ** level_of(seeds[8], (TOKENS, 2), ((0, 16),), -0.2, 0.2), 0.19921875, 0.796875).astype(jnp.bfloat16)
    norm_gain = jnp.clip(1.0 + 0.1 * jax.random.normal(seeds[9], (D,), jnp.float32), 0.5, 1.5).astype(jnp.bfloat16)
    w_gate = bell_draw(seeds[10], (EXPERTS, D, FF), D ** -0.5, 0.09375, ((0, 8), (2, 16)))
    w_up = bell_draw(seeds[11], (EXPERTS, D, FF), D ** -0.5, 0.09375, ((0, 8), (2, 16)))
    w_down = bell_draw(seeds[12], (EXPERTS, FF, D), FF ** -0.5, 0.046875, ((0, 8), (1, 16)))
    return dict(residual=residual, queries=queries, cache_keys=cache_keys, cache_values=cache_values, node_of_position=node_of_position, parent=parent, leaf_ids=leaf_ids, routes=routes, gate_weights=gate_weights, norm_gain=norm_gain, w_gate=w_gate, w_up=w_up, w_down=w_down)


def reference(residual, queries, cache_keys, cache_values, node_of_position, parent, leaf_ids, routes, gate_weights, norm_gain, w_gate, w_up, w_down):
    group_size = Q_HEADS // KV_HEADS
    score_scale = 1.0 / math.sqrt(HEAD_DIM)
    middle = parent[leaf_ids]
    upper = parent[middle]
    ancestors = jnp.stack([leaf_ids, middle, upper], axis=1)
    query_heads = queries.astype(jnp.float32).reshape(TOKENS, KV_HEADS, group_size, HEAD_DIM)
    key_blocks = cache_keys.reshape(N_DP, CACHE_DEV, KV_HEADS, HEAD_DIM)
    value_blocks = cache_values.reshape(N_DP, CACHE_DEV, KV_HEADS, HEAD_DIM)
    node_blocks = node_of_position.reshape(N_DP, CACHE_DEV)

    def one_owner(packed):
        keys_here, values_here, nodes_here = packed
        visible = jnp.any(nodes_here[None, :, None] == ancestors[:, None, :], axis=2)
        scores = jnp.einsum('tkgd,pkd->tkgp', query_heads, keys_here.astype(jnp.float32)) * score_scale
        scores = jnp.where(visible[:, None, None, :], scores, -jnp.inf)
        local_max = lax.optimization_barrier(jnp.max(scores, axis=3))
        exponent = jnp.exp(scores - local_max[..., None])
        local_total = lax.optimization_barrier(jnp.sum(exponent, axis=3))
        probs = exponent.astype(jnp.bfloat16)
        local_out = jnp.einsum('tkgp,pkd->tkgd', probs.astype(jnp.float32), values_here.astype(jnp.float32))
        return (local_max, local_total, local_out)
    maxima, totals, outputs = lax.map(one_owner, (key_blocks, value_blocks, node_blocks))
    global_max = lax.optimization_barrier(jnp.max(maxima, axis=0))
    factor = jnp.exp(maxima - global_max[None])
    attention = lax.optimization_barrier(jnp.sum(factor[..., None] * outputs, axis=0)) / lax.optimization_barrier(jnp.sum(factor * totals, axis=0))[..., None]
    attention = attention.reshape(TOKENS, D)
    attention_out = attention.astype(jnp.bfloat16)
    stream = (residual.astype(jnp.float32) + attention).astype(jnp.bfloat16)
    stream_wide = stream.astype(jnp.float32)
    inverse = lax.rsqrt(lax.optimization_barrier(jnp.mean(stream_wide * stream_wide, axis=1, keepdims=True)) + 1e-05)
    normed = (stream_wide * inverse * norm_gain.astype(jnp.float32)[None, :]).astype(jnp.bfloat16)
    flat_routes = routes.reshape(N_DP, ROWS_DP * 2)
    expert_hot = (flat_routes[:, :, None] == jnp.arange(EXPERTS, dtype=jnp.int32)[None, None, :]).astype(jnp.int32)
    slot_ranks = jnp.cumsum(expert_hot, axis=1) - expert_hot
    slot_ids = lax.optimization_barrier(jnp.sum(slot_ranks * expert_hot, axis=2)).reshape(-1)
    owner_rows = jnp.repeat(jnp.arange(N_DP, dtype=jnp.int32), ROWS_DP * 2)
    pair_tokens = jnp.repeat(jnp.arange(TOKENS, dtype=jnp.int32), 2)
    slot_index = (owner_rows * CAP + slot_ids).astype(jnp.int32)
    route_flat = flat_routes.reshape(-1)
    slot_table = jnp.full((EXPERTS, N_DP * CAP), TOKENS, dtype=jnp.int32)
    slot_table = slot_table.at[route_flat, slot_index].set(pair_tokens)
    normed_pad = jnp.concatenate([normed, jnp.zeros((1, D), jnp.bfloat16)], axis=0)

    def one_expert(packed):
        gate_mat, up_mat, down_mat, table_row = packed
        rows_in = jnp.take(normed_pad, table_row, axis=0)
        gate_val = jnp.dot(rows_in, gate_mat, preferred_element_type=jnp.float32)
        up_val = jnp.dot(rows_in, up_mat, preferred_element_type=jnp.float32)
        hidden = (jax.nn.silu(gate_val) * up_val).astype(jnp.bfloat16)
        return jnp.dot(hidden, down_mat, preferred_element_type=jnp.float32)
    expert_outputs = lax.map(one_expert, (w_gate, w_up, w_down, slot_table))
    picked = expert_outputs[route_flat, slot_index].reshape(TOKENS, 2, D)
    mixture = lax.optimization_barrier(jnp.sum(gate_weights.astype(jnp.float32)[:, :, None] * picked, axis=1))
    layer_out = (stream.astype(jnp.float32) + mixture).astype(jnp.bfloat16)
    return (attention_out, layer_out)
```

```python
import functools
import math

import jax
import jax.numpy as jnp
from jax import lax
from jax.experimental import pallas as pl
from jax.experimental.pallas import tpu as pltpu
from jax.sharding import PartitionSpec as P

HEAD_DIM = 128
EXPERTS = 8
CAP = 32
EPS = 1e-05
HIDE = -1e30
SCALE2 = math.log2(math.e) / math.sqrt(HEAD_DIM)
BF = jnp.bfloat16
F32 = jnp.float32


def ring_pairs(axis, shift):
    pairs = []
    for a in range(4):
        for b in range(4):
            if axis == 0:
                pairs.append((4 * a + b, 4 * ((a + shift) % 4) + b))
            else:
                pairs.append((4 * a + b, 4 * a + (b + shift) % 4))
    return pairs


def shift_dp(value, axis, shift):
    return lax.ppermute(value, "dp", ring_pairs(axis, shift))


def attend_kernel(order_ref, q0, q1, q2, q3, kt_ref, v_ref, out_ref, q_scr):
    step = pl.program_id(0)
    for k, ref in enumerate((q0, q1, q2, q3)):

        @pl.when(step // 4 == k)
        def _(ref=ref):
            q_scr[...] = ref[step % 4]

    bias = q_scr[:, 512:640]
    rows = [
        jnp.concatenate([q_scr[:, 128 * h : 128 * h + 128], bias], axis=1) for h in range(4)
    ]
    q_wide = jnp.concatenate(rows, axis=0)
    scores = jnp.dot(q_wide, kt_ref[...], preferred_element_type=F32)
    top = jnp.max(scores, axis=1, keepdims=True) * SCALE2
    top = top.astype(BF).astype(F32)
    probs = jnp.exp2(scores * SCALE2 - top).astype(BF)
    both = jnp.dot(probs, v_ref[...], preferred_element_type=F32)
    lane = lax.broadcasted_iota(jnp.int32, (64, 128), 1)
    stats = jnp.zeros((64, 128), F32)
    for h in range(4):
        part = both[64 * h : 64 * h + 64]
        out_ref[0, :, 128 * h : 128 * h + 128] = part[:, :128].astype(BF)
        total = part[:, 128:256]
        high = total.astype(BF).astype(F32)
        low = total - high
        stats = jnp.where(lane == h, top[64 * h : 64 * h + 64], stats)
        stats = jnp.where(lane == 4 + h, high, stats)
        stats = jnp.where(lane == 8 + h, low, stats)
    out_ref[0, :, 512:640] = stats.astype(BF)


def attend(order, blocks, kt_wide, v_wide):
    whole = lambda shape: pl.BlockSpec(shape, lambda g, order: tuple(0 for _ in shape))
    return pl.pallas_call(
        attend_kernel,
        out_shape=jax.ShapeDtypeStruct((16, 64, 640), BF),
        grid_spec=pltpu.PrefetchScalarGridSpec(
            num_scalar_prefetch=1,
            grid=(16,),
            in_specs=[whole((4, 64, 640)) for _ in range(4)]
            + [whole(kt_wide.shape), whole(v_wide.shape)],
            out_specs=pl.BlockSpec((1, 64, 640), lambda g, order: (order[g], 0, 0)),
            scratch_shapes=[pltpu.VMEM((64, 640), BF)],
        ),
        compiler_params=pltpu.CompilerParams(vmem_limit_bytes=40 << 20),
        name="attend",
    )(order, *blocks, kt_wide, v_wide)


def combine_kernel(got_ref, res_ref, disp_ref, att_ref, stream_ref, slot_ref):
    stats = got_ref[:, :, 512:640].astype(F32)
    top = jnp.max(stats, axis=0)
    factor = jnp.exp2(stats - top[None])
    for h in range(4):
        weight = factor[:, :, h : h + 1]
        total = stats[:, :, 4 + h : 5 + h] + stats[:, :, 8 + h : 9 + h]
        part = got_ref[:, :, 128 * h : 128 * h + 128].astype(F32)
        upper = jnp.sum(part * weight, axis=0)
        lower = jnp.sum(total * weight, axis=0)
        att = upper / lower
        cols = slice(128 * h, 128 * h + 128)
        att_ref[:, cols] = att.astype(BF)
        stream_ref[:, cols] = (res_ref[:, cols].astype(F32) + att).astype(BF)
    slot_ref[...] = jnp.dot(
        disp_ref[...], stream_ref[...], preferred_element_type=F32
    ).astype(BF)


def combine(got, residual, disp):
    return pl.pallas_call(
        combine_kernel,
        out_shape=(
            jax.ShapeDtypeStruct((64, 512), BF),
            jax.ShapeDtypeStruct((64, 512), BF),
            jax.ShapeDtypeStruct((256, 512), BF),
        ),
        name="combine",
    )(got, residual, disp)


def norm_kernel(x_ref, gain_ref, out_ref):
    total = jnp.zeros((32, 512), F32)
    for f in range(8):
        wide = x_ref[f].astype(F32)
        total = total + wide * wide
    mean = jnp.sum(total, axis=1, keepdims=True) * (1.0 / 4096.0)
    inverse = lax.rsqrt(mean + EPS)
    for f in range(8):
        cols = slice(512 * f, 512 * f + 512)
        out_ref[:, cols] = (x_ref[f].astype(F32) * inverse * gain_ref[:, cols].astype(F32)).astype(BF)


def norm(x, gain):
    return pl.pallas_call(
        norm_kernel,
        out_shape=jax.ShapeDtypeStruct((32, 4096), BF),
        name="norm",
    )(x, gain)


def moe_kernel(x_ref, wg_ref, wu_ref, wd_ref, out_ref, gate_acc, up_acc, hid):
    step = pl.program_id(0)

    @pl.when(step < 8)
    def _():
        x = x_ref[...]
        gate = jnp.dot(x, wg_ref[0], preferred_element_type=F32)
        up = jnp.dot(x, wu_ref[0], preferred_element_type=F32)

        @pl.when(step == 0)
        def _():
            gate_acc[...] = gate
            up_acc[...] = up

        @pl.when(step > 0)
        def _():
            gate_acc[...] += gate
            up_acc[...] += up

        @pl.when(step == 7)
        def _():
            g = gate_acc[...]
            hid[...] = (g / (1.0 + jnp.exp(-g)) * up_acc[...]).astype(BF)

    @pl.when(step >= 8)
    def _():
        out_ref[...] = jnp.dot(hid[...], wd_ref[0], preferred_element_type=F32).astype(BF)


def moe(x, w_gate, w_up, w_down):
    return pl.pallas_call(
        moe_kernel,
        out_shape=jax.ShapeDtypeStruct((512, 4096), BF),
        grid=(16,),
        in_specs=[
            pl.BlockSpec((512, 512), lambda i: (0, jnp.minimum(i, 7))),
            pl.BlockSpec((1, 512, 896), lambda i: (0, jnp.minimum(i, 7), 0)),
            pl.BlockSpec((1, 512, 896), lambda i: (0, jnp.minimum(i, 7), 0)),
            pl.BlockSpec((1, 896, 512), lambda i: (0, 0, jnp.maximum(i - 8, 0))),
        ],
        out_specs=pl.BlockSpec((512, 512), lambda i: (0, jnp.maximum(i - 8, 0))),
        scratch_shapes=[
            pltpu.VMEM((512, 896), F32),
            pltpu.VMEM((512, 896), F32),
            pltpu.VMEM((512, 896), BF),
        ],
        compiler_params=pltpu.CompilerParams(vmem_limit_bytes=40 << 20),
        name="moe",
    )(x, w_gate, w_up, w_down)


def add_kernel(x_ref, out_ref):
    total = jnp.zeros((32, 512), F32)
    for j in range(16):
        total = total + x_ref[j].astype(F32)
    out_ref[0] = total.astype(BF)


def add_up(x):
    return pl.pallas_call(
        add_kernel,
        out_shape=jax.ShapeDtypeStruct((8, 32, 512), BF),
        grid=(8,),
        in_specs=[pl.BlockSpec((16, 32, 512), lambda f: (0, 0, f))],
        out_specs=pl.BlockSpec((1, 32, 512), lambda f: (f, 0, 0)),
        name="add_up",
    )(x)


def finish_kernel(mix_ref, y_ref, stream_ref, out_ref):
    mixture = jnp.dot(mix_ref[...], y_ref[...], preferred_element_type=F32)
    out_ref[...] = (stream_ref[...].astype(F32) + mixture).astype(BF)


def finish(mix, y, stream):
    return pl.pallas_call(
        finish_kernel, out_shape=jax.ShapeDtypeStruct((64, 512), BF), name="finish"
    )(mix, y, stream)


def body(
    residual,
    queries,
    cache_keys,
    cache_values,
    node_of_position,
    parent,
    leaf_ids,
    routes,
    gate_weights,
    norm_gain,
    w_gate,
    w_up,
    w_down,
):
    rows = queries.shape[0]
    node_count = parent.shape[0]
    lane = jnp.arange(128, dtype=jnp.int32)
    leaf_hot = leaf_ids[:, None] == jnp.arange(node_count, dtype=jnp.int32)[None, :]
    middle = jnp.sum(jnp.where(leaf_hot, parent[None, :], 0), axis=1)
    middle_hot = middle[:, None] == jnp.arange(node_count, dtype=jnp.int32)[None, :]
    upper = jnp.sum(jnp.where(middle_hot, parent[None, :], 0), axis=1)
    seen = (
        (lane[None, :] == leaf_ids[:, None])
        | (lane[None, :] == middle[:, None])
        | (lane[None, :] == upper[:, None])
    )
    bias = jnp.where(seen, 0.0, HIDE).astype(BF)
    q_own = jnp.concatenate([queries, bias], axis=1)[None]
    stage = jnp.concatenate([q_own] + [shift_dp(q_own, 1, s) for s in (1, 2, 3)], axis=0)
    blocks = [stage] + [shift_dp(stage, 0, s) for s in (1, 2, 3)]

    kt_hot = (
        jnp.where(node_of_position < 0, 127, node_of_position)[None, :] == lane[:, None]
    ).astype(BF)
    kt_wide = jnp.concatenate([cache_keys.T, kt_hot], axis=0)
    v_wide = jnp.concatenate([cache_values, jnp.ones_like(cache_values)], axis=1)

    expert_range = jnp.arange(EXPERTS, dtype=jnp.int32)
    hot = routes[:, :, None] == expert_range[None, None, :]
    weight = jnp.sum(jnp.where(hot, gate_weights.astype(F32)[:, :, None], 0.0), axis=1)
    named = jnp.any(hot, axis=1)
    row = jnp.arange(rows, dtype=jnp.int32)
    before = (row[None, :] < row[:, None]).astype(BF)
    rank = jnp.dot(before, named.astype(BF), preferred_element_type=F32).astype(jnp.int32)
    slot = jnp.arange(CAP, dtype=jnp.int32)
    place = named.T[:, None, :] & (rank.T[:, None, :] == slot[None, :, None])
    disp = place.reshape(EXPERTS * CAP, rows).astype(BF)
    place_t = named[:, :, None] & (rank[:, :, None] == slot[None, None, :])
    mix = jnp.where(place_t, weight[:, :, None], 0.0).reshape(rows, EXPERTS * CAP).astype(BF)

    me = lax.axis_index("dp")
    rel = jnp.arange(16, dtype=jnp.int32)
    order = ((me // 4 - rel // 4) % 4) * 4 + (me % 4 - rel % 4) % 4
    partial = attend(order, blocks, kt_wide, v_wide)
    got = lax.all_to_all(partial, "dp", split_axis=0, concat_axis=0, tiled=True)
    attention_out, stream, slots = combine(got, residual, disp)

    mine = lax.all_to_all(slots.reshape(8, 32, 512), "expert", split_axis=0, concat_axis=0, tiled=True)
    normed = norm(mine, norm_gain[None, :])
    gathered = lax.all_gather(normed, "dp", axis=0, tiled=True)
    expert_y = moe(gathered, w_gate, w_up, w_down)
    spread = lax.all_to_all(
        expert_y.reshape(16, 32, 4096), "dp", split_axis=0, concat_axis=0, tiled=True
    )
    summed = add_up(spread)
    back = lax.all_to_all(summed, "expert", split_axis=0, concat_axis=0, tiled=True)
    layer_out = finish(mix, back.reshape(256, 512), stream)
    return (attention_out, layer_out)


def solution(mesh):
    in_specs = (
        P("dp", "expert"),
        P("dp", "expert"),
        P("dp", "expert"),
        P("dp", "expert"),
        P("dp"),
        P(),
        P("dp"),
        P("dp", None),
        P("dp", None),
        P(),
        P("expert", None, "dp"),
        P("expert", None, "dp"),
        P("expert", "dp", None),
    )
    out_specs = (P("dp", "expert"), P("dp", "expert"))
    return jax.shard_map(body, mesh=mesh, in_specs=in_specs, out_specs=out_specs, check_vma=False)
```

```python
import functools
import math

import jax
import jax.numpy as jnp
from jax import lax
from jax.experimental import pallas as pl
from jax.experimental.pallas import tpu as pltpu
from jax.sharding import PartitionSpec as P

HEAD_DIM = 128
EXPERTS = 8
CAP = 32
EPS = 1e-05
HIDE = -1e30
SCALE2 = math.log2(math.e) / math.sqrt(HEAD_DIM)
BF = jnp.bfloat16
F32 = jnp.float32


def ring_pairs(axis, shift):
    pairs = []
    for a in range(4):
        for b in range(4):
            if axis == 0:
                pairs.append((4 * a + b, 4 * ((a + shift) % 4) + b))
            else:
                pairs.append((4 * a + b, 4 * a + (b + shift) % 4))
    return pairs


def shift_dp(value, axis, shift):
    return lax.ppermute(value, "dp", ring_pairs(axis, shift))


def attend_kernel(order_ref, q0, q1, q2, q3, kt_ref, v_ref, out_ref, q_scr):
    step = pl.program_id(0)
    for k, ref in enumerate((q0, q1, q2, q3)):

        @pl.when(step // 2 == k)
        def _(ref=ref):
            q_scr[...] = ref[pl.ds(2 * (step % 2), 2)]

    lane = lax.broadcasted_iota(jnp.int32, (64, 128), 1)
    for b in range(2):
        bias = q_scr[b, :, 512:640]
        place = order_ref[2 * step + b]
        stats = jnp.zeros((64, 128), F32)
        for pair in range(2):
            rows = [
                jnp.concatenate([q_scr[b, :, 128 * h : 128 * h + 128], bias], axis=1)
                for h in (2 * pair, 2 * pair + 1)
            ]
            q_wide = jnp.concatenate(rows, axis=0)
            scores = jnp.dot(q_wide, kt_ref[...], preferred_element_type=F32)
            top = jnp.max(scores, axis=1, keepdims=True) * SCALE2
            top = top.astype(BF).astype(F32)
            probs = jnp.exp2(scores * SCALE2 - top).astype(BF)
            both = jnp.dot(probs, v_ref[...], preferred_element_type=F32)
            for k in range(2):
                h = 2 * pair + k
                part = both[64 * k : 64 * k + 64]
                out_ref[place, :, 128 * h : 128 * h + 128] = part[:, :128].astype(BF)
                total = part[:, 128:256]
                high = total.astype(BF).astype(F32)
                stats = jnp.where(lane == h, top[64 * k : 64 * k + 64], stats)
                stats = jnp.where(lane == 4 + h, high, stats)
                stats = jnp.where(lane == 8 + h, total - high, stats)
        out_ref[place, :, 512:640] = stats.astype(BF)


def attend(order, blocks, kt_wide, v_wide):
    whole = lambda shape: pl.BlockSpec(shape, lambda g, order: tuple(0 for _ in shape))
    return pl.pallas_call(
        attend_kernel,
        out_shape=jax.ShapeDtypeStruct((16, 64, 640), BF),
        grid_spec=pltpu.PrefetchScalarGridSpec(
            num_scalar_prefetch=1,
            grid=(8,),
            in_specs=[whole((4, 64, 640)) for _ in range(4)]
            + [whole(kt_wide.shape), whole(v_wide.shape)],
            out_specs=whole((16, 64, 640)),
            scratch_shapes=[pltpu.VMEM((2, 64, 640), BF)],
        ),
        compiler_params=pltpu.CompilerParams(vmem_limit_bytes=40 << 20),
        name="attend",
    )(order, *blocks, kt_wide, v_wide)


def combine_kernel(got_ref, res_ref, disp_ref, att_ref, stream_ref, slot_ref):
    stats = got_ref[:, :, 512:640].astype(F32)
    top = jnp.max(stats, axis=0)
    factor = jnp.exp2(stats - top[None])
    for h in range(4):
        weight = factor[:, :, h : h + 1]
        total = stats[:, :, 4 + h : 5 + h] + stats[:, :, 8 + h : 9 + h]
        part = got_ref[:, :, 128 * h : 128 * h + 128].astype(F32)
        upper = jnp.sum(part * weight, axis=0)
        lower = jnp.sum(total * weight, axis=0)
        att = upper / lower
        cols = slice(128 * h, 128 * h + 128)
        att_ref[:, cols] = att.astype(BF)
        stream_ref[:, cols] = (res_ref[:, cols].astype(F32) + att).astype(BF)
    slot_ref[...] = jnp.dot(
        disp_ref[...], stream_ref[...], preferred_element_type=F32
    ).astype(BF)


def combine(got, residual, disp):
    return pl.pallas_call(
        combine_kernel,
        out_shape=(
            jax.ShapeDtypeStruct((64, 512), BF),
            jax.ShapeDtypeStruct((64, 512), BF),
            jax.ShapeDtypeStruct((256, 512), BF),
        ),
        name="combine",
    )(got, residual, disp)


def norm_kernel(x_ref, gain_ref, low_ref, high_ref):
    total = jnp.zeros((32, 512), F32)
    for f in range(8):
        wide = x_ref[f].astype(F32)
        total = total + wide * wide
    mean = jnp.sum(total, axis=1, keepdims=True) * (1.0 / 4096.0)
    inverse = lax.rsqrt(mean + EPS)
    for f in range(8):
        gain = gain_ref[:, 512 * f : 512 * f + 512].astype(F32)
        value = (x_ref[f].astype(F32) * inverse * gain).astype(BF)
        half = low_ref if f < 4 else high_ref
        half[:, 512 * (f % 4) : 512 * (f % 4) + 512] = value


def norm(x, gain):
    return pl.pallas_call(
        norm_kernel,
        out_shape=(jax.ShapeDtypeStruct((32, 2048), BF), jax.ShapeDtypeStruct((32, 2048), BF)),
        name="norm",
    )(x, gain)


def hidden_kernel(*refs):
    low, high = refs[0:4], refs[4:8]
    wg_ref, wu_ref, out_ref, x_scr = refs[8:]

    @pl.when(pl.program_id(0) == 0)
    def _():
        for a in range(4):
            for b in range(4):
                r = 32 * (4 * a + b)
                x_scr[r : r + 32, :2048] = low[a][b]
                x_scr[r : r + 32, 2048:] = high[b][a]

    both = jnp.concatenate([wg_ref[0], wu_ref[0]], axis=1)
    result = jnp.dot(x_scr[...], both, preferred_element_type=F32)
    gate = result[:, :128]
    out_ref[...] = (gate / (1.0 + jnp.exp(-gate)) * result[:, 128:]).astype(BF)


def hidden_units(low, high, w_gate, w_up):
    part = pl.BlockSpec((4, 32, 2048), lambda i: (0, 0, 0), pipeline_mode=pl.Buffered(1))
    tile = pl.BlockSpec((1, 4096, 128), lambda i: (0, 0, i))
    return pl.pallas_call(
        hidden_kernel,
        out_shape=jax.ShapeDtypeStruct((512, 896), BF),
        grid=(7,),
        in_specs=[part] * 8 + [tile, tile],
        out_specs=pl.BlockSpec((512, 128), lambda i: (0, i)),
        scratch_shapes=[pltpu.VMEM((512, 4096), BF)],
        compiler_params=pltpu.CompilerParams(vmem_limit_bytes=40 << 20),
        name="hidden_units",
    )(*low, *high, w_gate, w_up)


def down_kernel(swap, h_ref, wd_ref, o0, o1, o2, o3, h_scr):
    @pl.when(pl.program_id(0) == 0)
    def _():
        for a in range(4):
            for b in range(4):
                r = 32 * (4 * a + b)
                t = 32 * (4 * b + a) if swap else r
                h_scr[t : t + 32] = h_ref[r : r + 32]

    result = jnp.dot(h_scr[...], wd_ref[0], preferred_element_type=F32)
    for k, ref in enumerate((o0, o1, o2, o3)):
        ref[...] = result[128 * k : 128 * k + 128].astype(BF)


def down(hidden, w_down, swap):
    offset = 4 if swap else 0
    return pl.pallas_call(
        functools.partial(down_kernel, swap),
        out_shape=[jax.ShapeDtypeStruct((128, 2048), BF)] * 4,
        grid=(4,),
        in_specs=[
            pl.BlockSpec((512, 896), lambda i: (0, 0)),
            pl.BlockSpec((1, 896, 512), lambda i: (0, 0, i + offset)),
        ],
        out_specs=[pl.BlockSpec((128, 512), lambda i: (0, i))] * 4,
        scratch_shapes=[pltpu.VMEM((512, 896), BF)],
        compiler_params=pltpu.CompilerParams(vmem_limit_bytes=40 << 20),
        name="down_high" if swap else "down_low",
    )(hidden, w_down)


def add_kernel(a, b, c, d, o0, o1, o2, o3):
    total = a[...].astype(F32) + b[...].astype(F32) + c[...].astype(F32) + d[...].astype(F32)
    for k, ref in enumerate((o0, o1, o2, o3)):
        ref[...] = total[32 * k : 32 * k + 32].astype(BF)


def add_first(parts):
    return pl.pallas_call(
        add_kernel,
        out_shape=[jax.ShapeDtypeStruct((32, 2048), BF)] * 4,
        grid=(2,),
        in_specs=[pl.BlockSpec((128, 1024), lambda i: (0, i))] * 4,
        out_specs=[pl.BlockSpec((32, 1024), lambda i: (0, i))] * 4,
        name="add_first",
    )(*parts)


def last_kernel(*refs):
    out_ref = refs[8]
    for half in range(2):
        a, b, c, d = refs[4 * half : 4 * half + 4]
        for f in range(4):
            cols = slice(512 * f, 512 * f + 512)
            total = (
                a[:, cols].astype(F32)
                + b[:, cols].astype(F32)
                + c[:, cols].astype(F32)
                + d[:, cols].astype(F32)
            )
            out_ref[4 * half + f] = total.astype(BF)


def add_last(low, high):
    return pl.pallas_call(
        last_kernel, out_shape=jax.ShapeDtypeStruct((8, 32, 512), BF), name="add_last"
    )(*low, *high)


def spread_near(value, axis):
    return [value] + [shift_dp(value, axis, s) for s in (1, 2, 3)]


def spread_far(near, axis):
    return [near] + [shift_dp(near, axis, s) for s in (1, 2, 3)]


def collect(parts, axis):
    return [parts[0]] + [shift_dp(parts[s], axis, -s) for s in (1, 2, 3)]


def finish_kernel(mix_ref, y_ref, stream_ref, out_ref):
    mixture = jnp.dot(mix_ref[...], y_ref[...], preferred_element_type=F32)
    out_ref[...] = (stream_ref[...].astype(F32) + mixture).astype(BF)


def finish(mix, y, stream):
    return pl.pallas_call(
        finish_kernel, out_shape=jax.ShapeDtypeStruct((64, 512), BF), name="finish"
    )(mix, y, stream)


def body(
    residual,
    queries,
    cache_keys,
    cache_values,
    node_of_position,
    parent,
    leaf_ids,
    routes,
    gate_weights,
    norm_gain,
    w_gate,
    w_up,
    w_down,
):
    rows = queries.shape[0]
    node_count = parent.shape[0]
    lane = jnp.arange(128, dtype=jnp.int32)
    leaf_hot = leaf_ids[:, None] == jnp.arange(node_count, dtype=jnp.int32)[None, :]
    middle = jnp.sum(jnp.where(leaf_hot, parent[None, :], 0), axis=1)
    middle_hot = middle[:, None] == jnp.arange(node_count, dtype=jnp.int32)[None, :]
    upper = jnp.sum(jnp.where(middle_hot, parent[None, :], 0), axis=1)
    seen = (
        (lane[None, :] == leaf_ids[:, None])
        | (lane[None, :] == middle[:, None])
        | (lane[None, :] == upper[:, None])
    )
    bias = jnp.where(seen, 0.0, HIDE).astype(BF)
    q_own = jnp.concatenate([queries, bias], axis=1)[None]
    stage = jnp.concatenate([q_own] + [shift_dp(q_own, 1, s) for s in (1, 2, 3)], axis=0)
    blocks = [stage] + [shift_dp(stage, 0, s) for s in (1, 2, 3)]

    kt_hot = (
        jnp.where(node_of_position < 0, 127, node_of_position)[None, :] == lane[:, None]
    ).astype(BF)
    kt_wide = jnp.concatenate([cache_keys.T, kt_hot], axis=0)
    v_wide = jnp.concatenate([cache_values, jnp.ones_like(cache_values)], axis=1)

    expert_range = jnp.arange(EXPERTS, dtype=jnp.int32)
    hot = routes[:, :, None] == expert_range[None, None, :]
    weight = jnp.sum(jnp.where(hot, gate_weights.astype(F32)[:, :, None], 0.0), axis=1)
    named = jnp.any(hot, axis=1)
    row = jnp.arange(rows, dtype=jnp.int32)
    before = (row[None, :] < row[:, None]).astype(BF)
    rank = jnp.dot(before, named.astype(BF), preferred_element_type=F32).astype(jnp.int32)
    slot = jnp.arange(CAP, dtype=jnp.int32)
    place = named.T[:, None, :] & (rank.T[:, None, :] == slot[None, :, None])
    disp = place.reshape(EXPERTS * CAP, rows).astype(BF)
    place_t = named[:, :, None] & (rank[:, :, None] == slot[None, None, :])
    mix = jnp.where(place_t, weight[:, :, None], 0.0).reshape(rows, EXPERTS * CAP).astype(BF)

    me = lax.axis_index("dp")
    rel = jnp.arange(16, dtype=jnp.int32)
    order = ((me // 4 - rel // 4) % 4) * 4 + (me % 4 - rel % 4) % 4
    partial = attend(order, blocks, kt_wide, v_wide)
    got = lax.all_to_all(partial, "dp", split_axis=0, concat_axis=0, tiled=True)
    attention_out, stream, slots = combine(got, residual, disp)

    mine = lax.all_to_all(slots.reshape(8, 32, 512), "expert", split_axis=0, concat_axis=0, tiled=True)
    low, high = norm(mine, norm_gain[None, :])
    low, high = lax.optimization_barrier((spread_near(low, 1), spread_near(high, 0)))
    low, high = spread_far(jnp.stack(low), 0), spread_far(jnp.stack(high), 1)
    hidden = hidden_units(low, high, w_gate, w_up)
    low = add_first(collect(down(hidden, w_down, False), 0))
    high = add_first(collect(down(hidden, w_down, True), 1))
    summed = add_last(collect(low, 1), collect(high, 0))
    back = lax.all_to_all(summed, "expert", split_axis=0, concat_axis=0, tiled=True)
    layer_out = finish(mix, back.reshape(256, 512), stream)
    return (attention_out, layer_out)


def solution(mesh):
    in_specs = (
        P("dp", "expert"),
        P("dp", "expert"),
        P("dp", "expert"),
        P("dp", "expert"),
        P("dp"),
        P(),
        P("dp"),
        P("dp", None),
        P("dp", None),
        P(),
        P("expert", None, "dp"),
        P("expert", None, "dp"),
        P("expert", "dp", None),
    )
    out_specs = (P("dp", "expert"), P("dp", "expert"))
    return jax.shard_map(body, mesh=mesh, in_specs=in_specs, out_specs=out_specs, check_vma=False)
```

```python
import functools
import math

import jax
import jax.numpy as jnp
from jax import lax
from jax.experimental import pallas as pl
from jax.experimental.pallas import tpu as pltpu
from jax.sharding import PartitionSpec as P

HEAD_DIM = 128
EXPERTS = 8
CAP = 32
EPS = 1e-05
HIDE = -1e30
SCALE2 = math.log2(math.e) / math.sqrt(HEAD_DIM)
BF = jnp.bfloat16
F32 = jnp.float32


def room(mib):
    return pltpu.CompilerParams(vmem_limit_bytes=mib << 20)


def ring_pairs(axis, shift):
    pairs = []
    for a in range(4):
        for b in range(4):
            if axis == 0:
                pairs.append((4 * a + b, 4 * ((a + shift) % 4) + b))
            else:
                pairs.append((4 * a + b, 4 * a + (b + shift) % 4))
    return pairs


def shift_dp(value, axis, shift):
    return lax.ppermute(value, "dp", ring_pairs(axis, shift))


def attend_kernel(q_ref, table_ref, kt_ref, v_ref, out_ref):
    lane = lax.broadcasted_iota(jnp.int32, (64, 128), 1)
    for b in range(2):
        leaf = q_ref[b, :, 512:640].astype(F32)
        leaf_hot = jnp.where(leaf == lane.astype(F32), 1.0, 0.0).astype(BF)
        bias = jnp.dot(leaf_hot, table_ref[...], preferred_element_type=F32).astype(BF)
        stats = jnp.zeros((64, 128), F32)
        for pair in range(2):
            rows = [
                jnp.concatenate([q_ref[b, :, 128 * h : 128 * h + 128], bias], axis=1)
                for h in (2 * pair, 2 * pair + 1)
            ]
            q_wide = jnp.concatenate(rows, axis=0)
            scores = jnp.dot(q_wide, kt_ref[...], preferred_element_type=F32)
            top = jnp.max(scores, axis=1, keepdims=True) * SCALE2
            top = top.astype(BF).astype(F32)
            probs = jnp.exp2(scores * SCALE2 - top).astype(BF)
            both = jnp.dot(probs, v_ref[...], preferred_element_type=F32)
            for k in range(2):
                h = 2 * pair + k
                part = both[64 * k : 64 * k + 64]
                out_ref[b, :, 128 * h : 128 * h + 128] = part[:, :128].astype(BF)
                total = part[:, 128:256]
                high = total.astype(BF).astype(F32)
                stats = jnp.where(lane == h, top[64 * k : 64 * k + 64], stats)
                stats = jnp.where(lane == 4 + h, high, stats)
                stats = jnp.where(lane == 8 + h, total - high, stats)
        out_ref[b, :, 512:640] = stats.astype(BF)


def attend(group, table, kt_wide, v_wide):
    whole = lambda shape: pl.BlockSpec(
        shape, lambda g: tuple(0 for _ in shape), pipeline_mode=pl.Buffered(1)
    )
    pair = pl.BlockSpec((2, 64, 640), lambda g: (g, 0, 0))
    return pl.pallas_call(
        attend_kernel,
        out_shape=jax.ShapeDtypeStruct((4, 64, 640), BF),
        grid=(2,),
        in_specs=[pair, whole(table.shape), whole(kt_wide.shape), whole(v_wide.shape)],
        out_specs=pair,
        compiler_params=room(16),
        name="attend",
    )(group, table, kt_wide, v_wide)


def merged(refs, pick):
    stats = [r[pick + (slice(512, 640),)].astype(F32) for r in refs]
    top = jnp.maximum(jnp.maximum(stats[0], stats[1]), jnp.maximum(stats[2], stats[3]))
    factor = [jnp.exp2(s - top) for s in stats]
    for h in range(4):
        cols = slice(128 * h, 128 * h + 128)
        upper = 0.0
        lower = 0.0
        for r, s, f in zip(refs, stats, factor):
            weight = f[:, h : h + 1]
            upper = upper + r[pick + (cols,)].astype(F32) * weight
            lower = lower + (s[:, 4 + h : 5 + h] + s[:, 8 + h : 9 + h]) * weight
        yield h, cols, top[:, h : h + 1], upper, lower


def merge_kernel(a, b, c, d, o0, o1, o2, o3):
    lane = lax.broadcasted_iota(jnp.int32, (64, 128), 1)
    for k, ref in enumerate((o0, o1, o2, o3)):
        stats = jnp.zeros((64, 128), F32)
        for h, cols, top, upper, lower in merged((a, b, c, d), (k, slice(None))):
            ref[:, cols] = upper.astype(BF)
            high = lower.astype(BF).astype(F32)
            stats = jnp.where(lane == h, top, stats)
            stats = jnp.where(lane == 4 + h, high, stats)
            stats = jnp.where(lane == 8 + h, lower - high, stats)
        ref[:, 512:640] = stats.astype(BF)


def merge(parts):
    return pl.pallas_call(
        merge_kernel,
        out_shape=[jax.ShapeDtypeStruct((64, 640), BF)] * 4,
        compiler_params=room(8),
        name="merge",
    )(*parts)


def combine_kernel(a, b, c, d, res_ref, disp_ref, att_ref, stream_ref, slot_ref):
    for h, cols, top, upper, lower in merged((a, b, c, d), (slice(None),)):
        att = upper / lower
        att_ref[:, cols] = att.astype(BF)
        stream_ref[:, cols] = (res_ref[:, cols].astype(F32) + att).astype(BF)
    slot_ref[...] = jnp.dot(
        disp_ref[...], stream_ref[...], preferred_element_type=F32
    ).astype(BF)


def combine(parts, residual, disp):
    return pl.pallas_call(
        combine_kernel,
        out_shape=(
            jax.ShapeDtypeStruct((64, 512), BF),
            jax.ShapeDtypeStruct((64, 512), BF),
            jax.ShapeDtypeStruct((256, 512), BF),
        ),
        compiler_params=room(8),
        name="combine",
    )(*parts, residual, disp)


def norm_kernel(x_ref, gain_ref, low_ref, high_ref):
    total = jnp.zeros((32, 512), F32)
    for f in range(8):
        wide = x_ref[f].astype(F32)
        total = total + wide * wide
    mean = jnp.sum(total, axis=1, keepdims=True) * (1.0 / 4096.0)
    inverse = lax.rsqrt(mean + EPS)
    for f in range(8):
        gain = gain_ref[:, 512 * f : 512 * f + 512].astype(F32)
        value = (x_ref[f].astype(F32) * inverse * gain).astype(BF)
        half = low_ref if f < 4 else high_ref
        half[:, 512 * (f % 4) : 512 * (f % 4) + 512] = value


def norm(x, gain):
    return pl.pallas_call(
        norm_kernel,
        out_shape=(jax.ShapeDtypeStruct((32, 2048), BF), jax.ShapeDtypeStruct((32, 2048), BF)),
        compiler_params=room(4),
        name="norm",
    )(x, gain)


def hidden_kernel(*refs):
    low, high = refs[0:4], refs[4:8]
    wg_ref, wu_ref, out_ref, x_scr = refs[8:]

    @pl.when(pl.program_id(0) == 0)
    def _():
        for a in range(4):
            for b in range(4):
                r = 32 * (4 * a + b)
                x_scr[r : r + 32, :2048] = low[a][b]
                x_scr[r : r + 32, 2048:] = high[b][a]

    both = jnp.concatenate([wg_ref[0], wu_ref[0]], axis=1)
    result = jnp.dot(x_scr[...], both, preferred_element_type=F32)
    gate = result[:, :128]
    out_ref[...] = (gate / (1.0 + jnp.exp(-gate)) * result[:, 128:]).astype(BF)


def hidden_units(low, high, w_gate, w_up):
    part = pl.BlockSpec((4, 32, 2048), lambda i: (0, 0, 0), pipeline_mode=pl.Buffered(1))
    tile = pl.BlockSpec((1, 4096, 128), lambda i: (0, 0, i))
    return pl.pallas_call(
        hidden_kernel,
        out_shape=jax.ShapeDtypeStruct((512, 896), BF),
        grid=(7,),
        in_specs=[part] * 8 + [tile, tile],
        out_specs=pl.BlockSpec((512, 128), lambda i: (0, i)),
        scratch_shapes=[pltpu.VMEM((512, 4096), BF)],
        compiler_params=room(20),
        name="hidden_units",
    )(*low, *high, w_gate, w_up)


def down_kernel(swap, h_ref, wd_ref, o0, o1, o2, o3, h_scr):
    @pl.when(pl.program_id(0) == 0)
    def _():
        for a in range(4):
            for b in range(4):
                r = 32 * (4 * a + b)
                t = 32 * (4 * b + a) if swap else r
                h_scr[t : t + 32] = h_ref[r : r + 32]

    result = jnp.dot(h_scr[...], wd_ref[0], preferred_element_type=F32)
    for k, ref in enumerate((o0, o1, o2, o3)):
        ref[...] = result[128 * k : 128 * k + 128].astype(BF)


def down(hidden, w_down, swap):
    offset = 4 if swap else 0
    return pl.pallas_call(
        functools.partial(down_kernel, swap),
        out_shape=[jax.ShapeDtypeStruct((128, 2048), BF)] * 4,
        grid=(4,),
        in_specs=[
            pl.BlockSpec((512, 896), lambda i: (0, 0)),
            pl.BlockSpec((1, 896, 512), lambda i: (0, 0, i + offset)),
        ],
        out_specs=[pl.BlockSpec((128, 512), lambda i: (0, i))] * 4,
        scratch_shapes=[pltpu.VMEM((512, 896), BF)],
        compiler_params=room(12),
        name="down_high" if swap else "down_low",
    )(hidden, w_down)


def add_kernel(a, b, c, d, o0, o1, o2, o3):
    total = a[...].astype(F32) + b[...].astype(F32) + c[...].astype(F32) + d[...].astype(F32)
    for k, ref in enumerate((o0, o1, o2, o3)):
        ref[...] = total[32 * k : 32 * k + 32].astype(BF)


def add_first(parts):
    return pl.pallas_call(
        add_kernel,
        out_shape=[jax.ShapeDtypeStruct((32, 2048), BF)] * 4,
        grid=(2,),
        in_specs=[pl.BlockSpec((128, 1024), lambda i: (0, i))] * 4,
        out_specs=[pl.BlockSpec((32, 1024), lambda i: (0, i))] * 4,
        compiler_params=room(8),
        name="add_first",
    )(*parts)


def last_kernel(*refs):
    out_ref = refs[8]
    for half in range(2):
        a, b, c, d = refs[4 * half : 4 * half + 4]
        for f in range(4):
            cols = slice(512 * f, 512 * f + 512)
            total = (
                a[:, cols].astype(F32)
                + b[:, cols].astype(F32)
                + c[:, cols].astype(F32)
                + d[:, cols].astype(F32)
            )
            out_ref[4 * half + f] = total.astype(BF)


def add_last(low, high):
    return pl.pallas_call(
        last_kernel,
        out_shape=jax.ShapeDtypeStruct((8, 32, 512), BF),
        compiler_params=room(8),
        name="add_last",
    )(*low, *high)


def spread_near(value, axis):
    return [value] + [shift_dp(value, axis, s) for s in (1, 2, 3)]


def spread_far(near, axis):
    return [near] + [shift_dp(near, axis, s) for s in (1, 2, 3)]


def collect(parts, axis):
    return [parts[0]] + [shift_dp(parts[s], axis, -s) for s in (1, 2, 3)]


def finish_kernel(mix_ref, y_ref, stream_ref, out_ref):
    mixture = jnp.dot(mix_ref[...], y_ref[...], preferred_element_type=F32)
    out_ref[...] = (stream_ref[...].astype(F32) + mixture).astype(BF)


def finish(mix, y, stream):
    return pl.pallas_call(
        finish_kernel,
        out_shape=jax.ShapeDtypeStruct((64, 512), BF),
        compiler_params=room(4),
        name="finish",
    )(mix, y, stream)


def body(
    residual,
    queries,
    cache_keys,
    cache_values,
    node_of_position,
    parent,
    leaf_ids,
    routes,
    gate_weights,
    norm_gain,
    w_gate,
    w_up,
    w_down,
):
    rows = queries.shape[0]
    node_count = parent.shape[0]
    leaf_wide = jnp.broadcast_to(leaf_ids.astype(BF)[:, None], (rows, 128))
    q_own = jnp.concatenate([queries, leaf_wide], axis=1)
    near = jnp.stack(spread_near(q_own, 1))
    groups = spread_far(near, 0)

    lane = jnp.arange(128, dtype=jnp.int32)
    node = jnp.arange(node_count, dtype=jnp.int32)
    middle_hot = parent[:, None] == node[None, :]
    upper = jnp.sum(jnp.where(middle_hot, parent[None, :], 0), axis=1)
    seen = (
        (lane[None, :] == node[:, None])
        | (lane[None, :] == parent[:, None])
        | (lane[None, :] == upper[:, None])
    )
    table = jnp.pad(jnp.where(seen, 0.0, HIDE).astype(BF), ((0, 128 - node_count), (0, 0)))

    kt_hot = (
        jnp.where(node_of_position < 0, 127, node_of_position)[None, :] == lane[:, None]
    ).astype(BF)
    kt_wide = jnp.concatenate([cache_keys.T, kt_hot], axis=0)
    v_wide = jnp.concatenate([cache_values, jnp.ones_like(cache_values)], axis=1)

    expert_range = jnp.arange(EXPERTS, dtype=jnp.int32)
    hot = routes[:, :, None] == expert_range[None, None, :]
    weight = jnp.sum(jnp.where(hot, gate_weights.astype(F32)[:, :, None], 0.0), axis=1)
    named = jnp.any(hot, axis=1)
    row = jnp.arange(rows, dtype=jnp.int32)
    before = (row[None, :] < row[:, None]).astype(BF)
    rank = jnp.dot(before, named.astype(BF), preferred_element_type=F32).astype(jnp.int32)
    slot = jnp.arange(CAP, dtype=jnp.int32)
    place = named.T[:, None, :] & (rank.T[:, None, :] == slot[None, :, None])
    disp = place.reshape(EXPERTS * CAP, rows).astype(BF)
    place_t = named[:, :, None] & (rank[:, :, None] == slot[None, None, :])
    mix = jnp.where(place_t, weight[:, :, None], 0.0).reshape(rows, EXPERTS * CAP).astype(BF)

    partial = [attend(groups[0], table, kt_wide, v_wide), None, None, None]
    partial[0], *groups[1:] = lax.optimization_barrier((partial[0], *groups[1:]))
    for turn in (1, 3, 2):
        partial[turn] = attend(groups[turn], table, kt_wide, v_wide)
    parts = collect(merge(collect(partial, 0)), 1)
    attention_out, stream, slots = combine(parts, residual, disp)

    mine = lax.all_to_all(slots.reshape(8, 32, 512), "expert", split_axis=0, concat_axis=0, tiled=True)
    low, high = norm(mine, norm_gain[None, :])
    low, high = lax.optimization_barrier((spread_near(low, 1), spread_near(high, 0)))
    low, high = spread_far(jnp.stack(low), 0), spread_far(jnp.stack(high), 1)
    hidden = hidden_units(low, high, w_gate, w_up)
    low = add_first(collect(down(hidden, w_down, False), 0))
    high = add_first(collect(down(hidden, w_down, True), 1))
    summed = add_last(collect(low, 1), collect(high, 0))
    back = lax.all_to_all(summed, "expert", split_axis=0, concat_axis=0, tiled=True)
    layer_out = finish(mix, back.reshape(256, 512), stream)
    return (attention_out, layer_out)


def solution(mesh):
    in_specs = (
        P("dp", "expert"),
        P("dp", "expert"),
        P("dp", "expert"),
        P("dp", "expert"),
        P("dp"),
        P(),
        P("dp"),
        P("dp", None),
        P("dp", None),
        P(),
        P("expert", None, "dp"),
        P("expert", None, "dp"),
        P("expert", "dp", None),
    )
    out_specs = (P("dp", "expert"), P("dp", "expert"))
    return jax.shard_map(body, mesh=mesh, in_specs=in_specs, out_specs=out_specs, check_vma=False)
```

```python
import functools
import math

import jax
import jax.numpy as jnp
from jax import lax
from jax.experimental import pallas as pl
from jax.experimental.pallas import tpu as pltpu
from jax.sharding import PartitionSpec as P

HEAD_DIM = 128
EXPERTS = 8
CAP = 32
EPS = 1e-05
HIDE = -1e30
FIRST_ROOM = 24
SCALE2 = math.log2(math.e) / math.sqrt(HEAD_DIM)
BF = jnp.bfloat16
F32 = jnp.float32


def room(mib):
    return pltpu.CompilerParams(vmem_limit_bytes=mib << 20)


def ring_pairs(axis, shift):
    pairs = []
    for a in range(4):
        for b in range(4):
            if axis == 0:
                pairs.append((4 * a + b, 4 * ((a + shift) % 4) + b))
            else:
                pairs.append((4 * a + b, 4 * a + (b + shift) % 4))
    return pairs


def shift_dp(value, axis, shift):
    return lax.ppermute(value, "dp", ring_pairs(axis, shift))


def attend_kernel(q_ref, table_ref, kt_ref, v_ref, out_ref):
    lane = lax.broadcasted_iota(jnp.int32, (64, 128), 1)
    for b in range(2):
        leaf = q_ref[b, :, 512:640].astype(F32)
        leaf_hot = jnp.where(leaf == lane.astype(F32), 1.0, 0.0).astype(BF)
        bias = jnp.dot(leaf_hot, table_ref[...], preferred_element_type=F32).astype(BF)
        stats = jnp.zeros((64, 128), F32)
        for pair in range(2):
            rows = [
                jnp.concatenate([q_ref[b, :, 128 * h : 128 * h + 128], bias], axis=1)
                for h in (2 * pair, 2 * pair + 1)
            ]
            q_wide = jnp.concatenate(rows, axis=0)
            scores = jnp.dot(q_wide, kt_ref[...], preferred_element_type=F32)
            top = jnp.max(scores, axis=1, keepdims=True) * SCALE2
            top = top.astype(BF).astype(F32)
            probs = jnp.exp2(scores * SCALE2 - top).astype(BF)
            both = jnp.dot(probs, v_ref[...], preferred_element_type=F32)
            for k in range(2):
                h = 2 * pair + k
                part = both[64 * k : 64 * k + 64]
                out_ref[b, :, 128 * h : 128 * h + 128] = part[:, :128].astype(BF)
                total = part[:, 128:256]
                high = total.astype(BF).astype(F32)
                stats = jnp.where(lane == h, top[64 * k : 64 * k + 64], stats)
                stats = jnp.where(lane == 4 + h, high, stats)
                stats = jnp.where(lane == 8 + h, total - high, stats)
        out_ref[b, :, 512:640] = stats.astype(BF)


def attend(group, table, kt_wide, v_wide):
    whole = lambda shape: pl.BlockSpec(
        shape, lambda g: tuple(0 for _ in shape), pipeline_mode=pl.Buffered(1)
    )
    pair = pl.BlockSpec((2, 64, 640), lambda g: (g, 0, 0))
    return pl.pallas_call(
        attend_kernel,
        out_shape=jax.ShapeDtypeStruct((4, 64, 640), BF),
        grid=(2,),
        in_specs=[pair, whole(table.shape), whole(kt_wide.shape), whole(v_wide.shape)],
        out_specs=pair,
        compiler_params=room(16),
        name="attend",
    )(group, table, kt_wide, v_wide)


def merged(refs, pick):
    stats = [r[pick + (slice(512, 640),)].astype(F32) for r in refs]
    top = jnp.maximum(jnp.maximum(stats[0], stats[1]), jnp.maximum(stats[2], stats[3]))
    factor = [jnp.exp2(s - top) for s in stats]
    for h in range(4):
        cols = slice(128 * h, 128 * h + 128)
        upper = 0.0
        lower = 0.0
        for r, s, f in zip(refs, stats, factor):
            weight = f[:, h : h + 1]
            upper = upper + r[pick + (cols,)].astype(F32) * weight
            lower = lower + (s[:, 4 + h : 5 + h] + s[:, 8 + h : 9 + h]) * weight
        yield h, cols, top[:, h : h + 1], upper, lower


def merge_kernel(a, b, c, d, o0, o1, o2, o3):
    lane = lax.broadcasted_iota(jnp.int32, (64, 128), 1)
    for k, ref in enumerate((o0, o1, o2, o3)):
        stats = jnp.zeros((64, 128), F32)
        for h, cols, top, upper, lower in merged((a, b, c, d), (k, slice(None))):
            ref[:, cols] = upper.astype(BF)
            high = lower.astype(BF).astype(F32)
            stats = jnp.where(lane == h, top, stats)
            stats = jnp.where(lane == 4 + h, high, stats)
            stats = jnp.where(lane == 8 + h, lower - high, stats)
        ref[:, 512:640] = stats.astype(BF)


def merge(parts):
    return pl.pallas_call(
        merge_kernel,
        out_shape=[jax.ShapeDtypeStruct((64, 640), BF)] * 4,
        compiler_params=room(8),
        name="merge",
    )(*parts)


def combine_kernel(a, b, c, d, res_ref, disp_ref, att_ref, stream_ref, slot_ref):
    for h, cols, top, upper, lower in merged((a, b, c, d), (slice(None),)):
        att = upper / lower
        att_ref[:, cols] = att.astype(BF)
        stream_ref[:, cols] = (res_ref[:, cols].astype(F32) + att).astype(BF)
    slot_ref[...] = jnp.dot(
        disp_ref[...], stream_ref[...], preferred_element_type=F32
    ).astype(BF)


def combine(parts, residual, disp):
    return pl.pallas_call(
        combine_kernel,
        out_shape=(
            jax.ShapeDtypeStruct((64, 512), BF),
            jax.ShapeDtypeStruct((64, 512), BF),
            jax.ShapeDtypeStruct((256, 512), BF),
        ),
        compiler_params=room(8),
        name="combine",
    )(*parts, residual, disp)


def norm_kernel(x_ref, gain_ref, low_ref, high_ref):
    total = jnp.zeros((32, 512), F32)
    for f in range(8):
        wide = x_ref[f].astype(F32)
        total = total + wide * wide
    mean = jnp.sum(total, axis=1, keepdims=True) * (1.0 / 4096.0)
    inverse = lax.rsqrt(mean + EPS)
    for f in range(8):
        gain = gain_ref[:, 512 * f : 512 * f + 512].astype(F32)
        value = (x_ref[f].astype(F32) * inverse * gain).astype(BF)
        half = low_ref if f < 4 else high_ref
        half[:, 512 * (f % 4) : 512 * (f % 4) + 512] = value


def norm(x, gain):
    return pl.pallas_call(
        norm_kernel,
        out_shape=(jax.ShapeDtypeStruct((32, 2048), BF), jax.ShapeDtypeStruct((32, 2048), BF)),
        compiler_params=room(4),
        name="norm",
    )(x, gain)


EARLY = [(a, b) for a in (0, 1, 3) for b in (0, 1, 3)]
LATE = [(a, b) for a in range(4) for b in range(4) if a == 2 or b == 2]


def gate_and_up(x_scr, both, out_ref):
    result = jnp.dot(x_scr[...], both, preferred_element_type=F32)
    gate = result[:, :128]
    out_ref[...] = (gate / (1.0 + jnp.exp(-gate)) * result[:, 128:]).astype(BF)


def first_kernel(l0, l1, l3, h0, h1, h3, wg_ref, wu_ref, out_ref, both_ref, x_scr):
    @pl.when(pl.program_id(0) == 0)
    def _():
        low, high = (l0, l1, None, l3), (h0, h1, None, h3)
        for k, (a, b) in enumerate(EARLY):
            rows = slice(32 * k, 32 * k + 32)
            x_scr[rows, :2048] = low[a][b]
            x_scr[rows, 2048:] = high[b][a]

    both = jnp.concatenate([wg_ref[0], wu_ref[0]], axis=1)
    both_ref[0] = both
    gate_and_up(x_scr, both, out_ref)


def second_kernel(l0, l1, l3, h0, h1, h3, la, lb, ha, hb, both_ref, out_ref, x_scr):
    @pl.when(pl.program_id(0) == 0)
    def _():
        low, high = (l0, l1, None, l3), (h0, h1, None, h3)
        low_far, high_far = (la, la, lb, lb), (ha, ha, hb, hb)
        for k, (a, b) in enumerate(LATE):
            rows = slice(32 * k, 32 * k + 32)
            x_scr[rows, :2048] = low_far[b][b % 2] if a == 2 else low[a][b]
            x_scr[rows, 2048:] = high_far[a][a % 2] if b == 2 else high[b][a]

    gate_and_up(x_scr, both_ref[0], out_ref)


def whole_once(shape):
    return pl.BlockSpec(shape, lambda i: tuple(0 for _ in shape), pipeline_mode=pl.Buffered(1))


def hidden_first(parts, w_gate, w_up):
    tile = pl.BlockSpec((1, 4096, 128), lambda i: (0, 0, i))
    return pl.pallas_call(
        first_kernel,
        out_shape=(
            jax.ShapeDtypeStruct((288, 896), BF),
            pltpu.VMEM((7, 4096, 256), BF),
        ),
        grid=(7,),
        in_specs=[whole_once(p.shape) for p in parts] + [tile, tile],
        out_specs=(
            pl.BlockSpec((288, 128), lambda i: (0, i)),
            pl.BlockSpec((1, 4096, 256), lambda i: (i, 0, 0)),
        ),
        scratch_shapes=[pltpu.VMEM((288, 4096), BF)],
        compiler_params=room(FIRST_ROOM),
        name="hidden_first",
    )(*parts, *[pltpu.with_memory_space_constraint(w, pltpu.HBM) for w in (w_gate, w_up)])


def hidden_second(parts, both):
    return pl.pallas_call(
        second_kernel,
        out_shape=jax.ShapeDtypeStruct((224, 896), BF),
        grid=(7,),
        in_specs=[whole_once(p.shape) for p in parts]
        + [pl.BlockSpec((1, 4096, 256), lambda i: (i, 0, 0))],
        out_specs=pl.BlockSpec((224, 128), lambda i: (0, i)),
        scratch_shapes=[pltpu.VMEM((224, 4096), BF)],
        compiler_params=room(16),
        name="hidden_second",
    )(*parts, pltpu.with_memory_space_constraint(both, pltpu.VMEM))


def down_kernel(swap, early_ref, late_ref, wd_ref, o0, o1, o2, o3, h_scr):
    @pl.when(pl.program_id(0) == 0)
    def _():
        for ref, places in ((early_ref, EARLY), (late_ref, LATE)):
            for k, (a, b) in enumerate(places):
                t = 32 * (4 * b + a) if swap else 32 * (4 * a + b)
                h_scr[t : t + 32] = ref[32 * k : 32 * k + 32]

    result = jnp.dot(h_scr[...], wd_ref[0], preferred_element_type=F32)
    for k, ref in enumerate((o0, o1, o2, o3)):
        ref[...] = result[128 * k : 128 * k + 128].astype(BF)


def down(early, late, w_down, swap):
    offset = 4 if swap else 0
    return pl.pallas_call(
        functools.partial(down_kernel, swap),
        out_shape=[jax.ShapeDtypeStruct((128, 2048), BF)] * 4,
        grid=(4,),
        in_specs=[
            whole_once(early.shape),
            whole_once(late.shape),
            pl.BlockSpec((1, 896, 512), lambda i: (0, 0, i + offset)),
        ],
        out_specs=[pl.BlockSpec((128, 512), lambda i: (0, i))] * 4,
        scratch_shapes=[pltpu.VMEM((512, 896), BF)],
        compiler_params=room(12),
        name="down_high" if swap else "down_low",
    )(early, late, w_down)


def add_kernel(a, b, c, d, o0, o1, o2, o3):
    total = a[...].astype(F32) + b[...].astype(F32) + c[...].astype(F32) + d[...].astype(F32)
    for k, ref in enumerate((o0, o1, o2, o3)):
        ref[...] = total[32 * k : 32 * k + 32].astype(BF)


def add_first(parts):
    return pl.pallas_call(
        add_kernel,
        out_shape=[jax.ShapeDtypeStruct((32, 2048), BF)] * 4,
        grid=(2,),
        in_specs=[pl.BlockSpec((128, 1024), lambda i: (0, i))] * 4,
        out_specs=[pl.BlockSpec((32, 1024), lambda i: (0, i))] * 4,
        compiler_params=room(8),
        name="add_first",
    )(*parts)


def last_kernel(*refs):
    out_ref = refs[8]
    for half in range(2):
        a, b, c, d = refs[4 * half : 4 * half + 4]
        for f in range(4):
            cols = slice(512 * f, 512 * f + 512)
            total = (
                a[:, cols].astype(F32)
                + b[:, cols].astype(F32)
                + c[:, cols].astype(F32)
                + d[:, cols].astype(F32)
            )
            out_ref[4 * half + f] = total.astype(BF)


def add_last(low, high):
    return pl.pallas_call(
        last_kernel,
        out_shape=jax.ShapeDtypeStruct((8, 32, 512), BF),
        compiler_params=room(8),
        name="add_last",
    )(*low, *high)


def spread_near(value, axis):
    return [value] + [shift_dp(value, axis, s) for s in (1, 2, 3)]


def spread_far(near, axis):
    return [near] + [shift_dp(near, axis, s) for s in (1, 2, 3)]


def collect(parts, axis):
    return [parts[0]] + [shift_dp(parts[s], axis, -s) for s in (1, 2, 3)]


def finish_kernel(mix_ref, y_ref, stream_ref, out_ref):
    mixture = jnp.dot(mix_ref[...], y_ref[...], preferred_element_type=F32)
    out_ref[...] = (stream_ref[...].astype(F32) + mixture).astype(BF)


def finish(mix, y, stream):
    return pl.pallas_call(
        finish_kernel,
        out_shape=jax.ShapeDtypeStruct((64, 512), BF),
        compiler_params=room(4),
        name="finish",
    )(mix, y, stream)


def body(
    residual,
    queries,
    cache_keys,
    cache_values,
    node_of_position,
    parent,
    leaf_ids,
    routes,
    gate_weights,
    norm_gain,
    w_gate,
    w_up,
    w_down,
):
    rows = queries.shape[0]
    node_count = parent.shape[0]
    leaf_wide = jnp.broadcast_to(leaf_ids.astype(BF)[:, None], (rows, 128))
    q_own = jnp.concatenate([queries, leaf_wide], axis=1)
    near = jnp.stack(spread_near(q_own, 1))
    groups = spread_far(near, 0)

    lane = jnp.arange(128, dtype=jnp.int32)
    node = jnp.arange(node_count, dtype=jnp.int32)
    middle_hot = parent[:, None] == node[None, :]
    upper = jnp.sum(jnp.where(middle_hot, parent[None, :], 0), axis=1)
    seen = (
        (lane[None, :] == node[:, None])
        | (lane[None, :] == parent[:, None])
        | (lane[None, :] == upper[:, None])
    )
    table = jnp.pad(jnp.where(seen, 0.0, HIDE).astype(BF), ((0, 128 - node_count), (0, 0)))

    kt_hot = (
        jnp.where(node_of_position < 0, 127, node_of_position)[None, :] == lane[:, None]
    ).astype(BF)
    kt_wide = jnp.concatenate([cache_keys.T, kt_hot], axis=0)
    v_wide = jnp.concatenate([cache_values, jnp.ones_like(cache_values)], axis=1)

    expert_range = jnp.arange(EXPERTS, dtype=jnp.int32)
    hot = routes[:, :, None] == expert_range[None, None, :]
    weight = jnp.sum(jnp.where(hot, gate_weights.astype(F32)[:, :, None], 0.0), axis=1)
    named = jnp.any(hot, axis=1)
    row = jnp.arange(rows, dtype=jnp.int32)
    before = (row[None, :] < row[:, None]).astype(BF)
    rank = jnp.dot(before, named.astype(BF), preferred_element_type=F32).astype(jnp.int32)
    slot = jnp.arange(CAP, dtype=jnp.int32)
    place = named.T[:, None, :] & (rank.T[:, None, :] == slot[None, :, None])
    disp = place.reshape(EXPERTS * CAP, rows).astype(BF)
    place_t = named[:, :, None] & (rank[:, :, None] == slot[None, None, :])
    mix = jnp.where(place_t, weight[:, :, None], 0.0).reshape(rows, EXPERTS * CAP).astype(BF)

    partial = [attend(groups[0], table, kt_wide, v_wide), None, None, None]
    partial[0], *groups[1:] = lax.optimization_barrier((partial[0], *groups[1:]))
    for turn in (1, 3, 2):
        partial[turn] = attend(groups[turn], table, kt_wide, v_wide)
    parts = collect(merge(collect(partial, 0)), 1)
    attention_out, stream, slots = combine(parts, residual, disp)

    mine = lax.all_to_all(slots.reshape(8, 32, 512), "expert", split_axis=0, concat_axis=0, tiled=True)
    low, high = norm(mine, norm_gain[None, :])
    low, high = lax.optimization_barrier((spread_near(low, 1), spread_near(high, 0)))
    low, high = jnp.stack(low), jnp.stack(high)
    low = [low, shift_dp(low, 0, 1), shift_dp(low, 0, -1)]
    high = [high, shift_dp(high, 1, 1), shift_dp(high, 1, -1)]
    low_far = [shift_dp(low[1][:2], 0, 1), shift_dp(low[2][2:], 0, -1)]
    high_far = [shift_dp(high[1][:2], 1, 1), shift_dp(high[2][2:], 1, -1)]
    parts = low + high
    early, both = hidden_first(parts, w_gate, w_up)
    parts = parts + low_far + high_far
    late = hidden_second(parts, both)
    low = add_first(collect(down(early, late, w_down, False), 0))
    high = add_first(collect(down(early, late, w_down, True), 1))
    summed = add_last(collect(low, 1), collect(high, 0))
    back = lax.all_to_all(summed, "expert", split_axis=0, concat_axis=0, tiled=True)
    layer_out = finish(mix, back.reshape(256, 512), stream)
    return (attention_out, layer_out)


def solution(mesh):
    in_specs = (
        P("dp", "expert"),
        P("dp", "expert"),
        P("dp", "expert"),
        P("dp", "expert"),
        P("dp"),
        P(),
        P("dp"),
        P("dp", None),
        P("dp", None),
        P(),
        P("expert", None, "dp"),
        P("expert", None, "dp"),
        P("expert", "dp", None),
    )
    out_specs = (P("dp", "expert"), P("dp", "expert"))
    return jax.shard_map(body, mesh=mesh, in_specs=in_specs, out_specs=out_specs, check_vma=False)
```

```python
import functools
import math

import jax
import jax.numpy as jnp
from jax import lax
from jax.experimental import pallas as pl
from jax.experimental.pallas import tpu as pltpu
from jax.sharding import PartitionSpec as P

HEAD_DIM = 128
EXPERTS = 8
CAP = 32
EPS = 1e-05
HIDE = -1e30
FIRST_ROOM = 24
SCALE2 = math.log2(math.e) / math.sqrt(HEAD_DIM)
BF = jnp.bfloat16
F32 = jnp.float32


def room(mib):
    return pltpu.CompilerParams(vmem_limit_bytes=mib << 20)


def ring_pairs(axis, shift):
    pairs = []
    for a in range(4):
        for b in range(4):
            if axis == 0:
                pairs.append((4 * a + b, 4 * ((a + shift) % 4) + b))
            else:
                pairs.append((4 * a + b, 4 * a + (b + shift) % 4))
    return pairs


def shift_dp(value, axis, shift):
    return lax.ppermute(value, "dp", ring_pairs(axis, shift))


def attend_kernel(q_ref, table_ref, kt_ref, v_ref, out_ref):
    lane = lax.broadcasted_iota(jnp.int32, (64, 128), 1)
    for b in range(2):
        leaf = q_ref[b, :, 512:640].astype(F32)
        leaf_hot = jnp.where(leaf == lane.astype(F32), 1.0, 0.0).astype(BF)
        bias = jnp.dot(leaf_hot, table_ref[...], preferred_element_type=F32).astype(BF)
        stats = jnp.zeros((64, 128), F32)
        for pair in range(2):
            rows = [
                jnp.concatenate([q_ref[b, :, 128 * h : 128 * h + 128], bias], axis=1)
                for h in (2 * pair, 2 * pair + 1)
            ]
            q_wide = jnp.concatenate(rows, axis=0)
            scores = jnp.dot(q_wide, kt_ref[...], preferred_element_type=F32)
            top = jnp.max(scores, axis=1, keepdims=True) * SCALE2
            top = top.astype(BF).astype(F32)
            probs = jnp.exp2(scores * SCALE2 - top).astype(BF)
            both = jnp.dot(probs, v_ref[...], preferred_element_type=F32)
            for k in range(2):
                h = 2 * pair + k
                part = both[64 * k : 64 * k + 64]
                out_ref[b, :, 128 * h : 128 * h + 128] = part[:, :128].astype(BF)
                total = part[:, 128:256]
                high = total.astype(BF).astype(F32)
                stats = jnp.where(lane == h, top[64 * k : 64 * k + 64], stats)
                stats = jnp.where(lane == 4 + h, high, stats)
                stats = jnp.where(lane == 8 + h, total - high, stats)
        out_ref[b, :, 512:640] = stats.astype(BF)


def attend(group, table, kt_wide, v_wide):
    whole = lambda shape: pl.BlockSpec(
        shape, lambda g: tuple(0 for _ in shape), pipeline_mode=pl.Buffered(1)
    )
    pair = pl.BlockSpec((2, 64, 640), lambda g: (g, 0, 0))
    return pl.pallas_call(
        attend_kernel,
        out_shape=jax.ShapeDtypeStruct((4, 64, 640), BF),
        grid=(2,),
        in_specs=[pair, whole(table.shape), whole(kt_wide.shape), whole(v_wide.shape)],
        out_specs=pair,
        compiler_params=room(16),
        name="attend",
    )(group, table, kt_wide, v_wide)


def merged(refs, pick):
    stats = [r[pick + (slice(512, 640),)].astype(F32) for r in refs]
    top = jnp.maximum(jnp.maximum(stats[0], stats[1]), jnp.maximum(stats[2], stats[3]))
    factor = [jnp.exp2(s - top) for s in stats]
    for h in range(4):
        cols = slice(128 * h, 128 * h + 128)
        upper = 0.0
        lower = 0.0
        for r, s, f in zip(refs, stats, factor):
            weight = f[:, h : h + 1]
            upper = upper + r[pick + (cols,)].astype(F32) * weight
            lower = lower + (s[:, 4 + h : 5 + h] + s[:, 8 + h : 9 + h]) * weight
        yield h, cols, top[:, h : h + 1], upper, lower


def merge_kernel(a, b, c, d, o0, o1, o2, o3):
    lane = lax.broadcasted_iota(jnp.int32, (64, 128), 1)
    for k, ref in enumerate((o0, o1, o2, o3)):
        stats = jnp.zeros((64, 128), F32)
        for h, cols, top, upper, lower in merged((a, b, c, d), (k, slice(None))):
            ref[:, cols] = upper.astype(BF)
            high = lower.astype(BF).astype(F32)
            stats = jnp.where(lane == h, top, stats)
            stats = jnp.where(lane == 4 + h, high, stats)
            stats = jnp.where(lane == 8 + h, lower - high, stats)
        ref[:, 512:640] = stats.astype(BF)


def merge(parts):
    return pl.pallas_call(
        merge_kernel,
        out_shape=[jax.ShapeDtypeStruct((64, 640), BF)] * 4,
        compiler_params=room(8),
        name="merge",
    )(*parts)


def combine_kernel(a, b, c, d, res_ref, disp_ref, att_ref, stream_ref, slot_ref):
    for h, cols, top, upper, lower in merged((a, b, c, d), (slice(None),)):
        att = upper / lower
        att_ref[:, cols] = att.astype(BF)
        stream_ref[:, cols] = (res_ref[:, cols].astype(F32) + att).astype(BF)
    slot_ref[...] = jnp.dot(
        disp_ref[...], stream_ref[...], preferred_element_type=F32
    ).astype(BF)


def combine(parts, residual, disp):
    return pl.pallas_call(
        combine_kernel,
        out_shape=(
            jax.ShapeDtypeStruct((64, 512), BF),
            jax.ShapeDtypeStruct((64, 512), BF),
            jax.ShapeDtypeStruct((256, 512), BF),
        ),
        compiler_params=room(8),
        name="combine",
    )(*parts, residual, disp)


def norm_kernel(x_ref, gain_ref, low_ref, high_ref):
    total = jnp.zeros((32, 512), F32)
    for f in range(8):
        wide = x_ref[f].astype(F32)
        total = total + wide * wide
    mean = jnp.sum(total, axis=1, keepdims=True) * (1.0 / 4096.0)
    inverse = lax.rsqrt(mean + EPS)
    for f in range(8):
        gain = gain_ref[:, 512 * f : 512 * f + 512].astype(F32)
        value = (x_ref[f].astype(F32) * inverse * gain).astype(BF)
        half = low_ref if f < 4 else high_ref
        half[:, 512 * (f % 4) : 512 * (f % 4) + 512] = value


def norm(x, gain):
    return pl.pallas_call(
        norm_kernel,
        out_shape=(jax.ShapeDtypeStruct((32, 2048), BF), jax.ShapeDtypeStruct((32, 2048), BF)),
        compiler_params=room(4),
        name="norm",
    )(x, gain)


EARLY = [(a, b) for a in (0, 1, 3) for b in (0, 1, 3)]
LATE = [(a, b) for a in range(4) for b in range(4) if a == 2 or b == 2]


def gate_and_up(x_scr, both, out_ref):
    result = jnp.dot(x_scr[...], both, preferred_element_type=F32)
    gate = result[:, :128]
    out_ref[...] = (gate / (1.0 + jnp.exp(-gate)) * result[:, 128:]).astype(BF)


def first_kernel(l0, l1, l3, h0, h1, h3, wg_ref, wu_ref, out_ref, both_ref, x_scr):
    @pl.when(pl.program_id(0) == 0)
    def _():
        low, high = (l0, l1, None, l3), (h0, h1, None, h3)
        for k, (a, b) in enumerate(EARLY):
            rows = slice(32 * k, 32 * k + 32)
            x_scr[rows, :2048] = low[a][b]
            x_scr[rows, 2048:] = high[b][a]

    both = jnp.concatenate([wg_ref[0], wu_ref[0]], axis=1)
    both_ref[0] = both
    gate_and_up(x_scr, both, out_ref)


def second_kernel(l0, l1, l3, h0, h1, h3, la, lb, ha, hb, both_ref, out_ref, x_scr):
    @pl.when(pl.program_id(0) == 0)
    def _():
        low, high = (l0, l1, None, l3), (h0, h1, None, h3)
        low_far, high_far = (la, la, lb, lb), (ha, ha, hb, hb)
        for k, (a, b) in enumerate(LATE):
            rows = slice(32 * k, 32 * k + 32)
            x_scr[rows, :2048] = low_far[b][b % 2] if a == 2 else low[a][b]
            x_scr[rows, 2048:] = high_far[a][a % 2] if b == 2 else high[b][a]

    gate_and_up(x_scr, both_ref[0], out_ref)


def whole_once(shape):
    return pl.BlockSpec(shape, lambda i: tuple(0 for _ in shape), pipeline_mode=pl.Buffered(1))


def hidden_first(parts, w_gate, w_up):
    tile = pl.BlockSpec((1, 4096, 128), lambda i: (0, 0, i))
    return pl.pallas_call(
        first_kernel,
        out_shape=(
            jax.ShapeDtypeStruct((288, 896), BF),
            pltpu.VMEM((7, 4096, 256), BF),
        ),
        grid=(7,),
        in_specs=[whole_once(p.shape) for p in parts] + [tile, tile],
        out_specs=(
            pl.BlockSpec((288, 128), lambda i: (0, i)),
            pl.BlockSpec((1, 4096, 256), lambda i: (i, 0, 0)),
        ),
        scratch_shapes=[pltpu.VMEM((288, 4096), BF)],
        compiler_params=room(FIRST_ROOM),
        name="hidden_first",
    )(*parts, *[pltpu.with_memory_space_constraint(w, pltpu.HBM) for w in (w_gate, w_up)])


def hidden_second(parts, both):
    return pl.pallas_call(
        second_kernel,
        out_shape=jax.ShapeDtypeStruct((224, 896), BF),
        grid=(7,),
        in_specs=[whole_once(p.shape) for p in parts]
        + [pl.BlockSpec((1, 4096, 256), lambda i: (i, 0, 0))],
        out_specs=pl.BlockSpec((224, 128), lambda i: (0, i)),
        scratch_shapes=[pltpu.VMEM((224, 4096), BF)],
        compiler_params=room(16),
        name="hidden_second",
    )(*parts, pltpu.with_memory_space_constraint(both, pltpu.VMEM))


def down_kernel(swap, early_ref, late_ref, wd_ref, o0, o1, o2, o3, h_scr):
    @pl.when(pl.program_id(0) == 0)
    def _():
        for ref, places in ((early_ref, EARLY), (late_ref, LATE)):
            for k, (a, b) in enumerate(places):
                t = 32 * (4 * b + a) if swap else 32 * (4 * a + b)
                h_scr[t : t + 32] = ref[32 * k : 32 * k + 32]

    result = jnp.dot(h_scr[...], wd_ref[0], preferred_element_type=F32)
    for k, ref in enumerate((o0, o1, o2, o3)):
        ref[...] = result[128 * k : 128 * k + 128].astype(BF)


def down(early, late, w_down, swap):
    offset = 4 if swap else 0
    return pl.pallas_call(
        functools.partial(down_kernel, swap),
        out_shape=[jax.ShapeDtypeStruct((128, 2048), BF)] * 4,
        grid=(4,),
        in_specs=[
            whole_once(early.shape),
            whole_once(late.shape),
            pl.BlockSpec((1, 896, 512), lambda i: (0, 0, i + offset)),
        ],
        out_specs=[pl.BlockSpec((128, 512), lambda i: (0, i))] * 4,
        scratch_shapes=[pltpu.VMEM((512, 896), BF)],
        compiler_params=room(12),
        name="down_high" if swap else "down_low",
    )(early, late, w_down)


def add_kernel(a, b, c, d, o0, o1, o2, o3):
    total = a[...].astype(F32) + b[...].astype(F32) + c[...].astype(F32) + d[...].astype(F32)
    for k, ref in enumerate((o0, o1, o2, o3)):
        ref[...] = total[32 * k : 32 * k + 32].astype(BF)


def add_first(parts):
    return pl.pallas_call(
        add_kernel,
        out_shape=[jax.ShapeDtypeStruct((32, 2048), BF)] * 4,
        grid=(2,),
        in_specs=[pl.BlockSpec((128, 1024), lambda i: (0, i))] * 4,
        out_specs=[pl.BlockSpec((32, 1024), lambda i: (0, i))] * 4,
        compiler_params=room(8),
        name="add_first",
    )(*parts)


def last_kernel(*refs):
    out_ref = refs[8]
    for half in range(2):
        a, b, c, d = refs[4 * half : 4 * half + 4]
        for f in range(4):
            cols = slice(512 * f, 512 * f + 512)
            total = (
                a[:, cols].astype(F32)
                + b[:, cols].astype(F32)
                + c[:, cols].astype(F32)
                + d[:, cols].astype(F32)
            )
            out_ref[4 * half + f] = total.astype(BF)


def add_last(low, high):
    return pl.pallas_call(
        last_kernel,
        out_shape=jax.ShapeDtypeStruct((8, 32, 512), BF),
        compiler_params=room(8),
        name="add_last",
    )(*low, *high)


def spread_near(value, axis):
    return [value] + [shift_dp(value, axis, s) for s in (1, 2, 3)]


def collect(parts, axis):
    return [parts[0]] + [shift_dp(parts[s], axis, -s) for s in (1, 2, 3)]


def finish_kernel(mix_ref, y_ref, stream_ref, out_ref):
    mixture = jnp.dot(mix_ref[...], y_ref[...], preferred_element_type=F32)
    out_ref[...] = (stream_ref[...].astype(F32) + mixture).astype(BF)


def finish(mix, y, stream):
    return pl.pallas_call(
        finish_kernel,
        out_shape=jax.ShapeDtypeStruct((64, 512), BF),
        compiler_params=room(4),
        name="finish",
    )(mix, y, stream)


def body(
    residual,
    queries,
    cache_keys,
    cache_values,
    node_of_position,
    parent,
    leaf_ids,
    routes,
    gate_weights,
    norm_gain,
    w_gate,
    w_up,
    w_down,
):
    rows = queries.shape[0]
    node_count = parent.shape[0]
    leaf_wide = jnp.broadcast_to(leaf_ids[:, None], (rows, 128)).astype(BF)
    q_own = jnp.concatenate([queries, leaf_wide], axis=1)
    near = jnp.stack(spread_near(q_own, 1))
    plus, minus = shift_dp(near, 0, 1), shift_dp(near, 0, -1)

    lane = jnp.arange(128, dtype=jnp.int32)
    node = jnp.arange(node_count, dtype=jnp.int32)
    middle_hot = parent[:, None] == node[None, :]
    upper = jnp.sum(jnp.where(middle_hot, parent[None, :], 0), axis=1)
    seen = (
        (lane[None, :] == node[:, None])
        | (lane[None, :] == parent[:, None])
        | (lane[None, :] == upper[:, None])
    )
    table = jnp.pad(jnp.where(seen, 0.0, HIDE).astype(BF), ((0, 128 - node_count), (0, 0)))

    kt_hot = (
        jnp.where(node_of_position < 0, 127, node_of_position)[None, :] == lane[:, None]
    ).astype(BF)
    kt_wide = jnp.concatenate([cache_keys.T, kt_hot], axis=0)
    v_wide = jnp.concatenate([cache_values, jnp.ones_like(cache_values)], axis=1)

    expert_range = jnp.arange(EXPERTS, dtype=jnp.int32)
    hot = routes[:, :, None] == expert_range[None, None, :]
    weight = jnp.sum(jnp.where(hot, gate_weights.astype(F32)[:, :, None], 0.0), axis=1)
    named = jnp.any(hot, axis=1)
    row = jnp.arange(rows, dtype=jnp.int32)
    before = (row[None, :] < row[:, None]).astype(BF)
    rank = jnp.dot(before, named.astype(BF), preferred_element_type=F32).astype(jnp.int32)
    slot = jnp.arange(CAP, dtype=jnp.int32)
    place = named.T[:, None, :] & (rank.T[:, None, :] == slot[None, :, None])
    disp = place.reshape(EXPERTS * CAP, rows).astype(BF)
    place_t = named[:, :, None] & (rank[:, :, None] == slot[None, None, :])
    mix = jnp.where(place_t, weight[:, :, None], 0.0).reshape(rows, EXPERTS * CAP).astype(BF)

    partial = [attend(near, table, kt_wide, v_wide), None, None, None]
    partial[0], plus, minus = lax.optimization_barrier((partial[0], plus, minus))
    far = (shift_dp(plus[:2], 0, 1), shift_dp(minus[2:], 0, -1))
    partial[1] = attend(plus, table, kt_wide, v_wide)
    partial[3] = attend(minus, table, kt_wide, v_wide)
    partial[2] = attend(jnp.concatenate(far, axis=0), table, kt_wide, v_wide)
    parts = collect(merge(collect(partial, 0)), 1)
    attention_out, stream, slots = combine(parts, residual, disp)

    mine = lax.all_to_all(slots.reshape(8, 32, 512), "expert", split_axis=0, concat_axis=0, tiled=True)
    low, high = norm(mine, norm_gain[None, :])
    low, high = lax.optimization_barrier((spread_near(low, 1), spread_near(high, 0)))
    low, high = jnp.stack(low), jnp.stack(high)
    low = [low, shift_dp(low, 0, 1), shift_dp(low, 0, -1)]
    high = [high, shift_dp(high, 1, 1), shift_dp(high, 1, -1)]
    low_far = [shift_dp(low[1][:2], 0, 1), shift_dp(low[2][2:], 0, -1)]
    high_far = [shift_dp(high[1][:2], 1, 1), shift_dp(high[2][2:], 1, -1)]
    parts = low + high
    early, both = hidden_first(parts, w_gate, w_up)
    parts = parts + low_far + high_far
    late = hidden_second(parts, both)
    low = add_first(collect(down(early, late, w_down, False), 0))
    high = add_first(collect(down(early, late, w_down, True), 1))
    summed = add_last(collect(low, 1), collect(high, 0))
    back = lax.all_to_all(summed, "expert", split_axis=0, concat_axis=0, tiled=True)
    layer_out = finish(mix, back.reshape(256, 512), stream)
    return (attention_out, layer_out)


def solution(mesh):
    in_specs = (
        P("dp", "expert"),
        P("dp", "expert"),
        P("dp", "expert"),
        P("dp", "expert"),
        P("dp"),
        P(),
        P("dp"),
        P("dp", None),
        P("dp", None),
        P(),
        P("expert", None, "dp"),
        P("expert", None, "dp"),
        P("expert", "dp", None),
    )
    out_specs = (P("dp", "expert"), P("dp", "expert"))
    return jax.shard_map(body, mesh=mesh, in_specs=in_specs, out_specs=out_specs, check_vma=False)
```

```python
import functools
import math

import jax
import jax.numpy as jnp
from jax import lax
from jax.experimental import pallas as pl
from jax.experimental.pallas import tpu as pltpu
from jax.sharding import PartitionSpec as P

HEAD_DIM = 128
EXPERTS = 8
CAP = 32
EPS = 1e-05
HIDE = -1e30
FIRST_ROOM = 24
SCALE2 = math.log2(math.e) / math.sqrt(HEAD_DIM)
BF = jnp.bfloat16
F32 = jnp.float32


def room(mib):
    return pltpu.CompilerParams(vmem_limit_bytes=mib << 20)


def ring_pairs(axis, shift):
    pairs = []
    for a in range(4):
        for b in range(4):
            if axis == 0:
                pairs.append((4 * a + b, 4 * ((a + shift) % 4) + b))
            else:
                pairs.append((4 * a + b, 4 * a + (b + shift) % 4))
    return pairs


def shift_dp(value, axis, shift):
    return lax.ppermute(value, "dp", ring_pairs(axis, shift))


def attend_kernel(q_ref, table_ref, kt_ref, v_ref, out_ref):
    lane = lax.broadcasted_iota(jnp.int32, (64, 128), 1)
    for b in range(2):
        leaf = q_ref[b, :, 512:640].astype(F32)
        leaf_hot = jnp.where(leaf == lane.astype(F32), 1.0, 0.0).astype(BF)
        bias = jnp.dot(leaf_hot, table_ref[...], preferred_element_type=F32).astype(BF)
        stats = jnp.zeros((64, 128), F32)
        for pair in range(2):
            rows = [
                jnp.concatenate([q_ref[b, :, 128 * h : 128 * h + 128], bias], axis=1)
                for h in (2 * pair, 2 * pair + 1)
            ]
            q_wide = jnp.concatenate(rows, axis=0)
            scores = jnp.dot(q_wide, kt_ref[...], preferred_element_type=F32)
            top = jnp.max(scores, axis=1, keepdims=True) * SCALE2
            top = top.astype(BF).astype(F32)
            probs = jnp.exp2(scores * SCALE2 - top).astype(BF)
            both = jnp.dot(probs, v_ref[...], preferred_element_type=F32)
            for k in range(2):
                h = 2 * pair + k
                part = both[64 * k : 64 * k + 64]
                out_ref[b, :, 128 * h : 128 * h + 128] = part[:, :128].astype(BF)
                total = part[:, 128:256]
                high = total.astype(BF).astype(F32)
                stats = jnp.where(lane == h, top[64 * k : 64 * k + 64], stats)
                stats = jnp.where(lane == 4 + h, high, stats)
                stats = jnp.where(lane == 8 + h, total - high, stats)
        out_ref[b, :, 512:640] = stats.astype(BF)


def attend(group, table, kt_wide, v_wide):
    whole = lambda shape: pl.BlockSpec(
        shape, lambda g: tuple(0 for _ in shape), pipeline_mode=pl.Buffered(1)
    )
    pair = pl.BlockSpec((2, 64, 640), lambda g: (g, 0, 0))
    return pl.pallas_call(
        attend_kernel,
        out_shape=jax.ShapeDtypeStruct((4, 64, 640), BF),
        grid=(2,),
        in_specs=[pair, whole(table.shape), whole(kt_wide.shape), whole(v_wide.shape)],
        out_specs=pair,
        compiler_params=room(16),
        name="attend",
    )(group, table, kt_wide, v_wide)


def merged(refs, pick):
    stats = [r[pick + (slice(512, 640),)].astype(F32) for r in refs]
    top = jnp.maximum(jnp.maximum(stats[0], stats[1]), jnp.maximum(stats[2], stats[3]))
    factor = [jnp.exp2(s - top) for s in stats]
    for h in range(4):
        cols = slice(128 * h, 128 * h + 128)
        upper = 0.0
        lower = 0.0
        for r, s, f in zip(refs, stats, factor):
            weight = f[:, h : h + 1]
            upper = upper + r[pick + (cols,)].astype(F32) * weight
            lower = lower + (s[:, 4 + h : 5 + h] + s[:, 8 + h : 9 + h]) * weight
        yield h, cols, top[:, h : h + 1], upper, lower


def merge_kernel(a, b, c, d, o0, o1, o2, o3):
    lane = lax.broadcasted_iota(jnp.int32, (64, 128), 1)
    for k, ref in enumerate((o0, o1, o2, o3)):
        stats = jnp.zeros((64, 128), F32)
        for h, cols, top, upper, lower in merged((a, b, c, d), (k, slice(None))):
            ref[:, cols] = upper.astype(BF)
            high = lower.astype(BF).astype(F32)
            stats = jnp.where(lane == h, top, stats)
            stats = jnp.where(lane == 4 + h, high, stats)
            stats = jnp.where(lane == 8 + h, lower - high, stats)
        ref[:, 512:640] = stats.astype(BF)


def merge(parts):
    return pl.pallas_call(
        merge_kernel,
        out_shape=[jax.ShapeDtypeStruct((64, 640), BF)] * 4,
        compiler_params=room(8),
        name="merge",
    )(*parts)


def combine_kernel(a, b, c, d, res_ref, disp_ref, att_ref, stream_ref, slot_ref):
    for h, cols, top, upper, lower in merged((a, b, c, d), (slice(None),)):
        att = upper / lower
        att_ref[:, cols] = att.astype(BF)
        stream_ref[:, cols] = (res_ref[:, cols].astype(F32) + att).astype(BF)
    slot_ref[...] = jnp.dot(
        disp_ref[...], stream_ref[...], preferred_element_type=F32
    ).astype(BF)


def combine(parts, residual, disp):
    return pl.pallas_call(
        combine_kernel,
        out_shape=(
            jax.ShapeDtypeStruct((64, 512), BF),
            jax.ShapeDtypeStruct((64, 512), BF),
            jax.ShapeDtypeStruct((256, 512), BF),
        ),
        compiler_params=room(8),
        name="combine",
    )(*parts, residual, disp)


def norm_kernel(x_ref, gain_ref, low_ref, high_ref):
    total = jnp.zeros((32, 512), F32)
    for f in range(8):
        wide = x_ref[f].astype(F32)
        total = total + wide * wide
    mean = jnp.sum(total, axis=1, keepdims=True) * (1.0 / 4096.0)
    inverse = lax.rsqrt(mean + EPS)
    for f in range(8):
        gain = gain_ref[:, 512 * f : 512 * f + 512].astype(F32)
        value = (x_ref[f].astype(F32) * inverse * gain).astype(BF)
        half = low_ref if f < 4 else high_ref
        half[:, 512 * (f % 4) : 512 * (f % 4) + 512] = value


def norm(x, gain):
    return pl.pallas_call(
        norm_kernel,
        out_shape=(jax.ShapeDtypeStruct((32, 2048), BF), jax.ShapeDtypeStruct((32, 2048), BF)),
        compiler_params=room(4),
        name="norm",
    )(x, gain)


EARLY = [(a, b) for a in (0, 1, 3) for b in (0, 1, 3)]
LATE = [(a, b) for a in range(4) for b in range(4) if a == 2 or b == 2]


def gate_and_up(x_scr, both, out_ref):
    result = jnp.dot(x_scr[...], both, preferred_element_type=F32)
    gate = result[:, :128]
    out_ref[...] = (gate / (1.0 + jnp.exp(-gate)) * result[:, 128:]).astype(BF)


def first_kernel(l0, l1, l3, h0, h1, h3, wg_ref, wu_ref, out_ref, both_ref, x_scr):
    @pl.when(pl.program_id(0) == 0)
    def _():
        low, high = (l0, l1, None, l3), (h0, h1, None, h3)
        for k, (a, b) in enumerate(EARLY):
            rows = slice(32 * k, 32 * k + 32)
            x_scr[rows, :2048] = low[a][b]
            x_scr[rows, 2048:] = high[b][a]

    both = jnp.concatenate([wg_ref[0], wu_ref[0]], axis=1)
    both_ref[0] = both
    gate_and_up(x_scr, both, out_ref)


def second_kernel(l0, l1, l3, h0, h1, h3, la, lb, ha, hb, both_ref, out_ref, x_scr):
    @pl.when(pl.program_id(0) == 0)
    def _():
        low, high = (l0, l1, None, l3), (h0, h1, None, h3)
        low_far, high_far = (la, la, lb, lb), (ha, ha, hb, hb)
        for k, (a, b) in enumerate(LATE):
            rows = slice(32 * k, 32 * k + 32)
            x_scr[rows, :2048] = low_far[b][b % 2] if a == 2 else low[a][b]
            x_scr[rows, 2048:] = high_far[a][a % 2] if b == 2 else high[b][a]

    gate_and_up(x_scr, both_ref[0], out_ref)


def whole_once(shape):
    return pl.BlockSpec(shape, lambda i: tuple(0 for _ in shape), pipeline_mode=pl.Buffered(1))


def hidden_first(parts, w_gate, w_up):
    tile = pl.BlockSpec((1, 4096, 128), lambda i: (0, 0, i))
    return pl.pallas_call(
        first_kernel,
        out_shape=(
            jax.ShapeDtypeStruct((288, 896), BF),
            pltpu.VMEM((7, 4096, 256), BF),
        ),
        grid=(7,),
        in_specs=[whole_once(p.shape) for p in parts] + [tile, tile],
        out_specs=(
            pl.BlockSpec((288, 128), lambda i: (0, i)),
            pl.BlockSpec((1, 4096, 256), lambda i: (i, 0, 0)),
        ),
        scratch_shapes=[pltpu.VMEM((288, 4096), BF)],
        compiler_params=room(FIRST_ROOM),
        name="hidden_first",
    )(*parts, *[pltpu.with_memory_space_constraint(w, pltpu.HBM) for w in (w_gate, w_up)])


def hidden_second(parts, both):
    return pl.pallas_call(
        second_kernel,
        out_shape=jax.ShapeDtypeStruct((224, 896), BF),
        grid=(7,),
        in_specs=[whole_once(p.shape) for p in parts]
        + [pl.BlockSpec((1, 4096, 256), lambda i: (i, 0, 0))],
        out_specs=pl.BlockSpec((224, 128), lambda i: (0, i)),
        scratch_shapes=[pltpu.VMEM((224, 4096), BF)],
        compiler_params=room(16),
        name="hidden_second",
    )(*parts, pltpu.with_memory_space_constraint(both, pltpu.VMEM))


def down_kernel(swap, early_ref, late_ref, wd_ref, o0, o1, o2, o3, h_scr):
    @pl.when(pl.program_id(0) == 0)
    def _():
        for ref, places in ((early_ref, EARLY), (late_ref, LATE)):
            for k, (a, b) in enumerate(places):
                t = 32 * (4 * b + a) if swap else 32 * (4 * a + b)
                h_scr[t : t + 32] = ref[32 * k : 32 * k + 32]

    result = jnp.dot(h_scr[...], wd_ref[0], preferred_element_type=F32)
    for k, ref in enumerate((o0, o1, o2, o3)):
        ref[...] = result[128 * k : 128 * k + 128].astype(BF)


def down(early, late, w_down, swap):
    offset = 2 if swap else 0
    return pl.pallas_call(
        functools.partial(down_kernel, swap),
        out_shape=[jax.ShapeDtypeStruct((128, 2048), BF)] * 4,
        grid=(2,),
        in_specs=[
            whole_once(early.shape),
            whole_once(late.shape),
            pl.BlockSpec((1, 896, 1024), lambda i: (0, 0, i + offset)),
        ],
        out_specs=[pl.BlockSpec((128, 1024), lambda i: (0, i))] * 4,
        scratch_shapes=[pltpu.VMEM((512, 896), BF)],
        compiler_params=room(14),
        name="down_high" if swap else "down_low",
    )(early, late, w_down)


def add_kernel(a, b, c, d, o0, o1, o2, o3):
    total = a[...].astype(F32) + b[...].astype(F32) + c[...].astype(F32) + d[...].astype(F32)
    for k, ref in enumerate((o0, o1, o2, o3)):
        ref[...] = total[32 * k : 32 * k + 32].astype(BF)


def add_first(parts):
    return pl.pallas_call(
        add_kernel,
        out_shape=[jax.ShapeDtypeStruct((32, 2048), BF)] * 4,
        grid=(2,),
        in_specs=[pl.BlockSpec((128, 1024), lambda i: (0, i))] * 4,
        out_specs=[pl.BlockSpec((32, 1024), lambda i: (0, i))] * 4,
        compiler_params=room(8),
        name="add_first",
    )(*parts)


def last_kernel(*refs):
    out_ref = refs[8]
    for half in range(2):
        a, b, c, d = refs[4 * half : 4 * half + 4]
        for f in range(4):
            cols = slice(512 * f, 512 * f + 512)
            total = (
                a[:, cols].astype(F32)
                + b[:, cols].astype(F32)
                + c[:, cols].astype(F32)
                + d[:, cols].astype(F32)
            )
            out_ref[4 * half + f] = total.astype(BF)


def add_last(low, high):
    return pl.pallas_call(
        last_kernel,
        out_shape=jax.ShapeDtypeStruct((8, 32, 512), BF),
        compiler_params=room(8),
        name="add_last",
    )(*low, *high)


def spread_near(value, axis):
    return [value] + [shift_dp(value, axis, s) for s in (1, 2, 3)]


def collect(parts, axis):
    return [parts[0]] + [shift_dp(parts[s], axis, -s) for s in (1, 2, 3)]


def finish_kernel(mix_ref, y_ref, stream_ref, out_ref):
    mixture = jnp.dot(mix_ref[...], y_ref[...], preferred_element_type=F32)
    out_ref[...] = (stream_ref[...].astype(F32) + mixture).astype(BF)


def finish(mix, y, stream):
    return pl.pallas_call(
        finish_kernel,
        out_shape=jax.ShapeDtypeStruct((64, 512), BF),
        compiler_params=room(4),
        name="finish",
    )(mix, y, stream)


def body(
    residual,
    queries,
    cache_keys,
    cache_values,
    node_of_position,
    parent,
    leaf_ids,
    routes,
    gate_weights,
    norm_gain,
    w_gate,
    w_up,
    w_down,
):
    rows = queries.shape[0]
    node_count = parent.shape[0]
    leaf_wide = jnp.broadcast_to(leaf_ids[:, None], (rows, 128)).astype(BF)
    q_own = jnp.concatenate([queries, leaf_wide], axis=1)
    near = jnp.stack(spread_near(q_own, 1))
    plus, minus = shift_dp(near, 0, 1), shift_dp(near, 0, -1)

    lane = jnp.arange(128, dtype=jnp.int32)
    node = jnp.arange(node_count, dtype=jnp.int32)
    middle_hot = parent[:, None] == node[None, :]
    upper = jnp.sum(jnp.where(middle_hot, parent[None, :], 0), axis=1)
    seen = (
        (lane[None, :] == node[:, None])
        | (lane[None, :] == parent[:, None])
        | (lane[None, :] == upper[:, None])
    )
    table = jnp.pad(jnp.where(seen, 0.0, HIDE).astype(BF), ((0, 128 - node_count), (0, 0)))

    kt_hot = (
        jnp.where(node_of_position < 0, 127, node_of_position)[None, :] == lane[:, None]
    ).astype(BF)
    kt_wide = jnp.concatenate([cache_keys.T, kt_hot], axis=0)
    v_wide = jnp.concatenate([cache_values, jnp.ones_like(cache_values)], axis=1)

    expert_range = jnp.arange(EXPERTS, dtype=jnp.int32)
    hot = routes[:, :, None] == expert_range[None, None, :]
    weight = jnp.sum(jnp.where(hot, gate_weights.astype(F32)[:, :, None], 0.0), axis=1)
    named = jnp.any(hot, axis=1)
    row = jnp.arange(rows, dtype=jnp.int32)
    before = (row[None, :] < row[:, None]).astype(BF)
    rank = jnp.dot(before, named.astype(BF), preferred_element_type=F32).astype(jnp.int32)
    slot = jnp.arange(CAP, dtype=jnp.int32)
    place = named.T[:, None, :] & (rank.T[:, None, :] == slot[None, :, None])
    disp = place.reshape(EXPERTS * CAP, rows).astype(BF)
    place_t = named[:, :, None] & (rank[:, :, None] == slot[None, None, :])
    mix = jnp.where(place_t, weight[:, :, None], 0.0).reshape(rows, EXPERTS * CAP).astype(BF)

    partial = [attend(near, table, kt_wide, v_wide), None, None, None]
    partial[0], plus, minus = lax.optimization_barrier((partial[0], plus, minus))
    far = (shift_dp(plus[:2], 0, 1), shift_dp(minus[2:], 0, -1))
    partial[1] = attend(plus, table, kt_wide, v_wide)
    partial[3] = attend(minus, table, kt_wide, v_wide)
    partial[2] = attend(jnp.concatenate(far, axis=0), table, kt_wide, v_wide)
    parts = collect(merge(collect(partial, 0)), 1)
    attention_out, stream, slots = combine(parts, residual, disp)

    mine = lax.all_to_all(slots.reshape(8, 32, 512), "expert", split_axis=0, concat_axis=0, tiled=True)
    low, high = norm(mine, norm_gain[None, :])
    low, high = lax.optimization_barrier((spread_near(low, 1), spread_near(high, 0)))
    low, high = jnp.stack(low), jnp.stack(high)
    low = [low, shift_dp(low, 0, 1), shift_dp(low, 0, -1)]
    high = [high, shift_dp(high, 1, 1), shift_dp(high, 1, -1)]
    low_far = [shift_dp(low[1][:2], 0, 1), shift_dp(low[2][2:], 0, -1)]
    high_far = [shift_dp(high[1][:2], 1, 1), shift_dp(high[2][2:], 1, -1)]
    parts = low + high
    early, both = hidden_first(parts, w_gate, w_up)
    parts = parts + low_far + high_far
    late = hidden_second(parts, both)
    low = add_first(collect(down(early, late, w_down, False), 0))
    high = add_first(collect(down(early, late, w_down, True), 1))
    summed = add_last(collect(low, 1), collect(high, 0))
    back = lax.all_to_all(summed, "expert", split_axis=0, concat_axis=0, tiled=True)
    layer_out = finish(mix, back.reshape(256, 512), stream)
    return (attention_out, layer_out)


def solution(mesh):
    in_specs = (
        P("dp", "expert"),
        P("dp", "expert"),
        P("dp", "expert"),
        P("dp", "expert"),
        P("dp"),
        P(),
        P("dp"),
        P("dp", None),
        P("dp", None),
        P(),
        P("expert", None, "dp"),
        P("expert", None, "dp"),
        P("expert", "dp", None),
    )
    out_specs = (P("dp", "expert"), P("dp", "expert"))
    return jax.shard_map(body, mesh=mesh, in_specs=in_specs, out_specs=out_specs, check_vma=False)
```
